256 devices in a mesh: tm: 16 (over z_hi, y), space: 16 (over z_lo, x, core).
Axes of the slice: x: 4, y: 4, z: 8 (z_hi: 4, z_lo: 2; z = z_hi * 2 + z_lo), core: 2. Of those that a mesh axis runs over, the one named last changes fastest.
Arguments:
- amplitude: float32 [160, 384, 512], P('tm', 'space'), may hold values from 0.3 to 3
- phase: float32 [160, 384, 512], P('tm', 'space'), may hold values from -3.140625 to 3.140625
- validity: int32 [384, 512], P('space'), may hold values 0 or 1
- iterations: int32 [16], P('tm'), may hold values from 10 to 20, as said below
- reference_date: int32 [16], P('tm'), may hold values from 0 to 9
Outputs:
- linked: float32 [2, 160, 384, 512], P(None, 'tm', 'space')
The draws below stay inside these ranges and needn't reach their ends.
Inputs may be any that keep to these rules, and one draw needn't show every extreme that they name: Every ministack takes between 10 and 20 iterations, and some ministack takes exactly 20.
All inputs are finite; a program needn't handle non-finite values. No bound on the sum of `validity` on one device may be relied on, other than what follows from the above.
Results may differ from the reference program's by a relative error of at most 0.0003.
Values sent between devices are 32-bit elements; how exact they have to be, the bound alone decides.
A program may use at most 64 MiB of HBM per device.

```python
import math
import jax
import jax.numpy as jnp
from jax import lax

DATES_MS = 10
WIN_ROWS = 11
WIN_COLS = 5
ITERS = 20
COLS = 512
MINISTACKS = 16
DATES = 160
ROWS = 384


def draw_iterations(key, part):
    first_key, second_key = jax.random.split(jax.random.fold_in(key, 7))
    counts = jax.random.randint(first_key, (MINISTACKS,), ITERS // 2, ITERS + 1)
    chosen = jax.random.randint(second_key, (), 0, MINISTACKS)
    return jnp.where(jnp.arange(MINISTACKS) == chosen, ITERS, counts).astype(jnp.int32)


def plant(values, rng, least, high):
    dims = values.shape
    spot = [jax.random.randint(jax.random.fold_in(rng, axis), (), 0, dims[axis]) for axis in range(len(dims))]
    values = values.at[tuple(spot)].set(least)
    longest = dims.index(max(dims))
    spot[longest] = (spot[longest] + 1) % dims[longest]
    return values.at[tuple(spot)].set(high)


def levels(own_key, extent, cuts, low, largest):
    level = 1.0
    for axis_at, blocks in cuts:
        steps = jax.random.uniform(jax.random.fold_in(jax.random.fold_in(own_key, 6), axis_at), (blocks,), jnp.float32, low / len(cuts), largest / len(cuts))
        level = level * jnp.repeat(jnp.exp(steps), extent[axis_at] // blocks).reshape((-1,) + (1,) * (len(extent) - 1 - axis_at))
    return level


def setup_inputs(seed: int = 0) -> dict:
    seeds = jax.random.split(jax.random.key(seed), 6)
    return {
        "amplitude": jnp.clip(jnp.exp(math.log(3.0) - 2.3025851 * jax.random.uniform(seeds[0], (DATES, ROWS, COLS), jnp.float32) ** levels(seeds[0], (DATES, ROWS, COLS), ((0, 16), (1, 16)), -0.2, 0.2)), 0.3, 3.0),
        "phase": jnp.clip(jax.random.uniform(seeds[1], (DATES, ROWS, COLS), jnp.float32, -3.140625, 3.140625), -3.140625, 3.140625),
        "validity": plant((jax.random.randint(seeds[2], (ROWS, COLS), 0, 8) < 7).astype(jnp.int32), jax.random.fold_in(seeds[2], 1), 0, 1),
        "iterations": draw_iterations(jax.random.fold_in(seeds[5], 71), 0),
        "reference_date": plant(jax.random.randint(seeds[4], (MINISTACKS,), 0, DATES_MS), jax.random.fold_in(seeds[4], 1), 0, DATES_MS - 1).astype(jnp.int32),
    }


masked_weight = 0.125
link_floor = 0.03

def box_valid(values):
    out_rows = values.shape[-2] - WIN_ROWS + 1
    row_sums = values[..., 0:out_rows, :]
    for offset in range(1, WIN_ROWS):
        row_sums = row_sums + values[..., offset:offset + out_rows, :]
    out_cols = values.shape[-1] - WIN_COLS + 1
    summed = row_sums[..., 0:out_cols]
    for offset in range(1, WIN_COLS):
        summed = summed + row_sums[..., offset:offset + out_cols]
    return summed

def estimate(window_block, sweep_limit):
    date_count = (window_block.shape[0] - 1) // 2
    amplitudes = window_block[:date_count]
    angles = window_block[date_count:2 * date_count]
    weights = window_block[2 * date_count]
    real_part = amplitudes * jnp.cos(angles)
    imag_part = amplitudes * jnp.sin(angles)
    cross_real = weights * (real_part[:, None] * real_part[None] + imag_part[:, None] * imag_part[None])
    cross_imag = weights * (imag_part[:, None] * real_part[None] - real_part[:, None] * imag_part[None])
    power_real = box_valid(cross_real)
    power_imag = box_valid(cross_imag)
    own_power = box_valid(weights * amplitudes * amplitudes)
    inverse = 1.0 / jnp.sqrt(own_power)
    coher_real = power_real * inverse[:, None] * inverse[None]
    coher_imag = power_imag * inverse[:, None] * inverse[None]
    start_real = jnp.full(own_power.shape, 1.0 / math.sqrt(date_count), jnp.float32)
    start_imag = jnp.zeros(own_power.shape, jnp.float32)

    def power_step(turn_no, vectors):
        old_real, old_imag = vectors
        new_real = lax.optimization_barrier(jnp.sum(coher_real * old_real[None] - coher_imag * old_imag[None], axis=1)) + old_real
        new_imag = lax.optimization_barrier(jnp.sum(coher_real * old_imag[None] + coher_imag * old_real[None], axis=1)) + old_imag
        length = jnp.sqrt(lax.optimization_barrier(jnp.sum(new_real * new_real + new_imag * new_imag, axis=0)))
        active = turn_no < sweep_limit
        return (jnp.where(active, new_real / length, old_real), jnp.where(active, new_imag / length, old_imag))
    vec_real, vec_imag = lax.fori_loop(0, ITERS, power_step, (start_real, start_imag))
    half_rows = WIN_ROWS // 2
    half_cols = WIN_COLS // 2
    inner_real = real_part[:, half_rows:real_part.shape[1] - half_rows, half_cols:real_part.shape[2] - half_cols]
    inner_imag = imag_part[:, half_rows:imag_part.shape[1] - half_rows, half_cols:imag_part.shape[2] - half_cols]
    comp_real = lax.optimization_barrier(jnp.sum(vec_real * inner_real + vec_imag * inner_imag, axis=0))
    comp_imag = lax.optimization_barrier(jnp.sum(vec_real * inner_imag - vec_imag * inner_real, axis=0))
    return (vec_real, vec_imag, comp_real, comp_imag)

def link_phases(stacked, sweep_limit):
    columns = stacked.shape[2]
    half_cols = WIN_COLS // 2
    padded = jnp.pad(stacked, ((0, 0), (0, 0), (half_cols, half_cols)))
    block_cols = min(128, columns)
    blocks = columns // block_cols

    def one_block(block_no):
        window = lax.dynamic_slice_in_dim(padded, block_no * block_cols, block_cols + 2 * half_cols, 2)
        return estimate(window, sweep_limit)
    results = lax.map(one_block, jnp.arange(blocks, dtype=jnp.int32))

    def merge_cols(pieces):
        placed = jnp.moveaxis(pieces, 0, -2)
        return placed.reshape(placed.shape[:-2] + (columns,))
    return tuple((merge_cols(result) for result in results))

def refer_dates(vec_real, vec_imag, chosen):
    date_count = vec_real.shape[0]
    picked = (jnp.arange(date_count, dtype=jnp.int32) == chosen).astype(jnp.float32)[:, None, None]
    ref_real = lax.optimization_barrier(jnp.sum(vec_real * picked, axis=0))
    ref_imag = lax.optimization_barrier(jnp.sum(vec_imag * picked, axis=0))
    linked_real = date_count * (vec_real * ref_real + vec_imag * ref_imag)
    linked_imag = date_count * (vec_imag * ref_real - vec_real * ref_imag)
    return (linked_real, linked_imag)

def pad_columns(values):
    half_cols = WIN_COLS // 2
    return jnp.pad(values, [(0, 0)] * (values.ndim - 1) + [(half_cols, half_cols)])

def link_offsets(comp_real, comp_imag, next_real, next_imag, weights):
    cross_real = box_valid(pad_columns(weights * (comp_real * next_real + comp_imag * next_imag)))
    cross_imag = box_valid(pad_columns(weights * (comp_imag * next_real - comp_real * next_imag)))
    own_power = box_valid(pad_columns(weights * (comp_real * comp_real + comp_imag * comp_imag)))
    next_power = box_valid(pad_columns(weights * (next_real * next_real + next_imag * next_imag)))
    denominator = jnp.sqrt((own_power + 1.0) * (next_power + 1.0))
    off_real = cross_real / denominator
    off_imag = cross_imag / denominator
    magnitude = jnp.sqrt(off_real * off_real + off_imag * off_imag)
    bounded = jnp.maximum(magnitude, link_floor)
    return (off_real / bounded, off_imag / bounded)

def reference(amplitude, phase, validity, iterations, reference_date):
    date_count = DATES_MS
    half_rows = WIN_ROWS // 2
    row_count = amplitude.shape[1]
    columns = amplitude.shape[2]
    weights = jnp.where(validity == 1, 1.0, masked_weight).astype(jnp.float32)
    amp_stacks = amplitude.reshape(MINISTACKS, date_count, row_count, columns)
    phase_stacks = phase.reshape(MINISTACKS, date_count, row_count, columns)

    def one_stack(inputs):
        amp_block, phase_block, sweep_limit, chosen = inputs
        stacked = jnp.concatenate([amp_block, phase_block, weights[None]], axis=0)
        stacked = jnp.pad(stacked, ((0, 0), (half_rows, half_rows), (0, 0)))
        vec_real, vec_imag, comp_real, comp_imag = link_phases(stacked, sweep_limit)
        linked_real, linked_imag = refer_dates(vec_real, vec_imag, chosen)
        return (linked_real, linked_imag, comp_real, comp_imag)
    linked_real, linked_imag, comp_real, comp_imag = lax.map(one_stack, (amp_stacks, phase_stacks, iterations, reference_date))
    next_real = jnp.concatenate([comp_real[1:], jnp.zeros_like(comp_real[:1])], axis=0)
    next_imag = jnp.concatenate([comp_imag[1:], jnp.zeros_like(comp_imag[:1])], axis=0)

    def pad_rows(values):
        return jnp.pad(values, [(0, 0)] * (values.ndim - 2) + [(half_rows, half_rows), (0, 0)])
    unit_real, unit_imag = link_offsets(pad_rows(comp_real), pad_rows(comp_imag), pad_rows(next_real), pad_rows(next_imag), pad_rows(weights))

    def chain_step(vectors, link):
        datum_real, datum_imag = vectors
        link_real, link_imag = link
        following = (datum_real * link_real - datum_imag * link_imag, datum_real * link_imag + datum_imag * link_real)
        return (following, vectors)
    start = (jnp.ones((row_count, columns), jnp.float32), jnp.zeros((row_count, columns), jnp.float32))
    final_state, datums = lax.scan(chain_step, start, (unit_real, unit_imag))
    datum_real = datums[0][:, None]
    datum_imag = datums[1][:, None]
    out_real = linked_real * datum_real - linked_imag * datum_imag
    out_imag = linked_real * datum_imag + linked_imag * datum_real
    return jnp.stack([out_real, out_imag]).reshape(2, MINISTACKS * date_count, row_count, columns)
```

```python
import jax
import jax.numpy as jnp
from jax import lax
from jax.experimental import pallas as pl
from jax.experimental.pallas import tpu as pltpu
from jax.sharding import PartitionSpec as P

MESH = pl.DeviceIdType.MESH
DATES = 10
REACH = 5
FOLD = 12
EXT = FOLD + 2 * REACH
ROWS = 2 * FOLD
TILES = ROWS // 8
MASKED = 0.125
FLOOR = 0.03
F32 = jnp.float32

SIN = (1.0, -1.0 / 6, 1.0 / 120, -1.0 / 5040, 1.0 / 362880, -1.0 / 39916800)
COS = (1.0, -1.0 / 2, 1.0 / 24, -1.0 / 720, 1.0 / 40320, -1.0 / 3628800, 1.0 / 479001600)


def horner(terms, x):
    total = terms[-1] * x + terms[-2]
    for term in terms[-3::-1]:
        total = total * x + term
    return total


def phasor(amplitude, phase):
    half = 0.5 * phase
    square = half * half
    sine = horner(SIN, square) * half
    cosine = horner(COS, square)
    twice = sine + sine
    return amplitude - amplitude * (twice * sine), amplitude * (twice * cosine)


def sublanes():
    return lax.broadcasted_iota(jnp.int32, (8, 128), 0)


def lanes():
    return lax.broadcasted_iota(jnp.int32, (8, 128), 1)


def column_sum():
    lane, block = lanes(), sublanes() & 3
    not_first = jnp.where(block > 0, 1.0, 0.0).astype(F32)
    not_last = jnp.where(block < 3, 1.0, 0.0).astype(F32)
    edges = [(amount, lane >= 128 - amount, lane < amount) for amount in (1, 2)]

    def apply(x):
        before = pltpu.roll(x, 1, 0) * not_first
        after = pltpu.roll(x, 7, 0) * not_last
        total = x
        for amount, high, low in edges:
            total = total + pltpu.roll(jnp.where(high, before, x), amount, 1)
            total = total + pltpu.roll(jnp.where(low, after, x), 128 - amount, 1)
        return total

    return apply


def row_sums(values):
    tails = [None] * 11
    tails[10] = values[10]
    for r in range(9, -1, -1):
        tails[r] = tails[r + 1] + values[r]
    out = [tails[0]]
    head = values[11]
    for r in range(1, 11):
        out.append(tails[r] + head)
        head = head + values[r + 11]
    out.append(head)
    return out


def halo_kernel(amp, pha, val, zr, zi, wt, A, B, V, local, send, recv):
    count = lax.axis_size("space")
    me = lax.axis_index("space")
    up, down = lax.rem(me + count - 1, count), lax.rem(me + 1, count)
    arrays = ((amp, A), (pha, B), (val, V))

    def lead(source):
        return (slice(None),) * (len(source.shape) - 4)

    for k, (source, target) in enumerate(arrays):
        all_ = lead(source)
        for r in range(FOLD + REACH):
            for half, row in ((0, r), (1, ROWS - 1 - r)):
                pltpu.make_async_copy(
                    source.at[all_ + (row // 8, slice(None), row % 8)],
                    target.at[all_ + (REACH + r, pl.ds(4 * half, 4))],
                    local.at[k],
                ).start()

    barrier = pltpu.get_barrier_semaphore()
    for neighbour in (up, down):
        pl.semaphore_signal(barrier, inc=1, device_id={"space": neighbour}, device_id_type=MESH)
    pl.semaphore_wait(barrier, 2)

    for k, (source, target) in enumerate(arrays):
        all_ = lead(source)
        for r in range(REACH):
            for half, row, to in ((0, ROWS - 1 - r, down), (1, r, up)):
                pltpu.make_async_remote_copy(
                    source.at[all_ + (row // 8, slice(None), row % 8)],
                    target.at[all_ + (REACH - 1 - r, pl.ds(4 * half, 4))],
                    send.at[k, half],
                    recv.at[k, half],
                    device_id={"space": to},
                    device_id_type=MESH,
                ).start()

    for k, (source, target) in enumerate(arrays):
        own = target.at[lead(source) + (pl.ds(REACH, FOLD + REACH),)]
        pltpu.make_async_copy(own, own, local.at[k]).wait()

    def phasors(first, last):
        def one(d, carry):
            for p in range(first, last):
                real, imag = phasor(A[d, p], B[d, p])
                zr[d, p] = real
                zi[d, p] = imag
            return carry

        lax.fori_loop(0, DATES, one, 0)

    phasors(REACH, EXT)
    for p in range(REACH, EXT):
        wt[p] = jnp.where(V[p] == 1, 1.0, MASKED).astype(F32)

    for k, (source, target) in enumerate(arrays):
        for half in range(2):
            edge = target.at[lead(source) + (pl.ds(0, REACH), pl.ds(4 * half, 4))]
            pltpu.make_async_copy(edge, edge, send.at[k, half]).wait()
            pltpu.make_async_copy(edge, edge, recv.at[k, half]).wait()

    phasors(0, REACH)
    above = jnp.where(me > 0, 1.0, 0.0).astype(F32)
    below = jnp.where(me < count - 1, 1.0, 0.0).astype(F32)
    inside = jnp.where(sublanes() < 4, above, below)
    for p in range(REACH):
        wt[p] = jnp.where(V[p] == 1, 1.0, MASKED).astype(F32) * inside


def main_kernel(iterations, chosen, zr, zi, wt, linked, comp, wr, wi, inv, R, I, S, QR, QI, QS, QD, vec):
    columns = column_sum()

    def own_power(d, carry):
        values = [wt[p] * (zr[d, p] * zr[d, p] + zi[d, p] * zi[d, p]) for p in range(EXT)]
        for r, total in enumerate(row_sums(values)):
            inv[d, r] = 0.5 * lax.rsqrt(columns(total))
        return carry

    lax.fori_loop(0, DATES, own_power, 0)

    def first_date(i, carry):
        for p in range(EXT):
            wr[p] = wt[p] * zr[i, p]
            wi[p] = wt[p] * zi[i, p]

        def second_date(j, carry):
            real, imag = [], []
            for p in range(EXT):
                a, b, c, d = wr[p], wi[p], zr[j, p], zi[j, p]
                real.append(a * c + b * d)
                imag.append(b * c - a * d)
            real, imag = row_sums(real), row_sums(imag)
            for r in range(FOLD):
                scale = inv[i, r] * inv[j, r]
                x = columns(real[r]) * scale
                y = columns(imag[r]) * scale
                R[r, i * DATES + j] = x
                I[r, i * DATES + j] = y
                S[r, i * DATES + j] = x + y
                S[r, j * DATES + i] = x - y
            return carry

        return lax.fori_loop(i + 1, DATES, second_date, carry)

    lax.fori_loop(0, DATES - 1, first_date, 0)

    n = iterations[0]
    odd = (n & 1) == 1
    turns = (n - 1) >> 1
    ref = chosen[0]

    def flat(i, j):
        return i * DATES + j

    def upper(i, j):
        return flat(min(i, j), max(i, j))

    def row_total(real, imag, diagonal):
        out_r, out_i = [], []
        for i in range(DATES):
            tr, ti = diagonal(i), None
            for j in range(DATES):
                if j == i:
                    continue
                tr = tr + real(upper(i, j))
                value = imag(upper(i, j))
                if ti is None:
                    ti = value if i < j else -value
                else:
                    ti = ti + value if i < j else ti - value
            out_r.append(tr)
            out_i.append(ti)
        return out_r, out_i

    def position(r, carry):
        squares = [jnp.full((8, 128), 0.25, F32) for _ in range(DATES)]
        for i in range(DATES):
            for j in range(i + 1, DATES):
                k = flat(i, j)
                x, y = R[r, k], I[r, k]
                size = x * x + y * y
                squares[i] = squares[i] + size
                squares[j] = squares[j] + size
        for i in range(DATES):
            QD[i] = squares[i]
        for i in range(DATES):
            for j in range(i + 1, DATES):
                rr, ii, mixed = None, None, None
                for k in range(DATES):
                    if k == i or k == j:
                        continue
                    a = R[r, upper(i, k)] * R[r, upper(j, k)]
                    b = I[r, upper(i, k)] * I[r, upper(j, k)]
                    c = S[r, flat(i, k)] * S[r, flat(k, j)]
                    same = (i < k) == (j < k)
                    rr = a if rr is None else rr + a
                    if ii is None:
                        ii = b if same else -b
                    else:
                        ii = ii + b if same else ii - b
                    mixed = c if mixed is None else mixed + c
                k = flat(i, j)
                x = R[r, k] + (rr + ii)
                y = I[r, k] + (mixed - (rr - ii))
                QR[k] = x
                QI[k] = y
                QS[k] = x + y
                QS[flat(j, i)] = x - y

        one_r, one_i = row_total(lambda k: R[r, k], lambda k: I[r, k], lambda i: jnp.full((8, 128), 0.5, F32))
        two_r, two_i = row_total(lambda k: QR[k], lambda k: QI[k], lambda i: QD[i])
        start = [jnp.where(odd, a, b) for a, b in zip(one_r + one_i, two_r + two_i)]

        def turn(_, v):
            vr, vi = v[:DATES], v[DATES:]
            both = [a + b for a, b in zip(vr, vi)]
            out_r, out_i = [], []
            for i in range(DATES):
                d = QD[i]
                rr, ii, mixed = None, None, None
                for j in range(DATES):
                    if j == i:
                        continue
                    a = QR[upper(i, j)] * vr[j]
                    b = QI[upper(i, j)] * vi[j]
                    c = QS[flat(i, j)] * both[j]
                    rr = a if rr is None else rr + a
                    if ii is None:
                        ii = b if i < j else -b
                    else:
                        ii = ii + b if i < j else ii - b
                    mixed = c if mixed is None else mixed + c
                out_r.append(d * vr[i] + (rr - ii))
                out_i.append(d * vi[i] + (mixed - (rr + ii)))
            return out_r + out_i

        v = lax.fori_loop(0, turns, turn, start)
        total = None
        for x in v:
            total = x * x if total is None else total + x * x
        scale = lax.rsqrt(total)
        v = [x * scale for x in v]
        vr, vi = v[:DATES], v[DATES:]
        for t in range(2 * DATES):
            vec[t] = v[t]
        cr, ci = None, None
        for t in range(DATES):
            a, b = zr[t, r + REACH], zi[t, r + REACH]
            x = vr[t] * a + vi[t] * b
            y = vr[t] * b - vi[t] * a
            cr = x if cr is None else cr + x
            ci = y if ci is None else ci + y
        comp[0, r] = cr
        comp[1, r] = ci
        ref_r, ref_i = DATES * vec[ref], DATES * vec[DATES + ref]
        for t in range(DATES):
            x = vr[t] * ref_r + vi[t] * ref_i
            y = vi[t] * ref_r - vr[t] * ref_i
            for part, value in ((t, x), (DATES + t, y)):
                for half, row in ((0, r), (1, ROWS - 1 - r)):
                    first = (row >> 3) * 32 + (row & 7)
                    linked[part, pl.ds(first, 4, stride=8), :] = value[4 * half : 4 * half + 4]
        return carry

    lax.fori_loop(0, FOLD, position, 0)


def link_kernel(comp, wt, datum, near, own_edge, near_edge, u, got, ready, dat, sem, send_u, recv_u, send_d, recv_d):
    stacks, spaces = lax.axis_size("tm"), lax.axis_size("space")
    m, s = lax.axis_index("tm"), lax.axis_index("space")
    before, after = lax.rem(m + stacks - 1, stacks), lax.rem(m + 1, stacks)
    up, down = lax.rem(s + spaces - 1, spaces), lax.rem(s + 1, spaces)

    barrier = pltpu.get_barrier_semaphore()

    def greet(tm, space):
        pl.semaphore_signal(barrier, inc=1, device_id={"tm": tm, "space": space}, device_id_type=MESH)

    for step in range(1, stacks):
        greet(lax.rem(m + step, stacks), s)
    for space in (up, down):
        greet(m, space)
        greet(before, space)
        greet(after, space)
    pl.semaphore_wait(barrier, stacks - 1 + 6)

    heads, tails = pl.ds(0, 4), pl.ds(4, 4)
    edge = pl.ds(0, REACH)
    plan = (
        (comp, near, (before, s)),
        (comp.at[:, edge, tails], own_edge.at[:, :, heads], (m, down)),
        (comp.at[:, edge, heads], own_edge.at[:, :, tails], (m, up)),
        (comp.at[:, edge, tails], near_edge.at[:, :, heads], (before, down)),
        (comp.at[:, edge, heads], near_edge.at[:, :, tails], (before, up)),
    )
    copies = []
    for k, (source, target, (tm, space)) in enumerate(plan):
        copy = pltpu.make_async_remote_copy(
            source, target, sem.at[0, k], sem.at[1, k], device_id={"tm": tm, "space": space}, device_id_type=MESH
        )
        copy.start()
        copies.append(copy)
    for copy in copies:
        copy.wait()

    def extended(block, edges, part):
        rows = [edges[part, REACH - 1 - k] for k in range(REACH)]
        rows += [block[part, r] for r in range(FOLD)]
        rows += [pltpu.roll(block[part, FOLD - 1 - k], 4, 0) for k in range(REACH)]
        return rows

    ar, ai = extended(comp, own_edge, 0), extended(comp, own_edge, 1)
    br, bi = extended(near, near_edge, 0), extended(near, near_edge, 1)
    columns = column_sum()
    cross_r, cross_i, power_a, power_b = [], [], [], []
    for p in range(EXT):
        w = wt[p]
        xr, xi = w * ar[p], w * ai[p]
        cross_r.append(xr * br[p] + xi * bi[p])
        cross_i.append(xi * br[p] - xr * bi[p])
        power_a.append(xr * ar[p] + xi * ai[p])
        power_b.append(w * (br[p] * br[p] + bi[p] * bi[p]))
    cross_r, cross_i, power_a, power_b = [row_sums(x) for x in (cross_r, cross_i, power_a, power_b)]
    for r in range(FOLD):
        scale = lax.rsqrt((columns(power_a[r]) + 1.0) * (columns(power_b[r]) + 1.0))
        x, y = columns(cross_r[r]) * scale, columns(cross_i[r]) * scale
        bounded = lax.rsqrt(jnp.maximum(x * x + y * y, FLOOR * FLOOR))
        u[r, 0] = x * bounded
        u[r, 1] = y * bounded

    def u_copy(step):
        to = lax.rem(m + step, stacks)
        return to, pltpu.make_async_remote_copy(
            u.at[to], got.at[m], send_u.at[to], recv_u.at[m], device_id={"tm": to}, device_id_type=MESH
        )

    for step in range(1, stacks):
        to = lax.rem(m + step, stacks)

        @pl.when(to < FOLD)
        def _():
            u_copy(step)[1].start()

    @pl.when(m < FOLD)
    def _():
        got[m] = u[m]
        xr, xi = jnp.ones((8, 128), F32), jnp.zeros((8, 128), F32)
        for k in range(stacks):
            ready[k, 0] = xr
            ready[k, 1] = xi

            @pl.when(k != m)
            def _():
                pltpu.make_async_remote_copy(
                    ready.at[k], dat.at[m], send_d.at[k], recv_d.at[m], device_id={"tm": k}, device_id_type=MESH
                ).start()

            @pl.when(k != m)
            def _():
                pltpu.make_async_copy(got.at[k], got.at[k], recv_u.at[k]).wait()

            lr, li = got[k, 0], got[k, 1]
            xr, xi = xr * lr - xi * li, xr * li + xi * lr
        dat[m] = ready[m]

    for r in range(FOLD):

        @pl.when(r != m)
        def _():
            pltpu.make_async_copy(dat.at[r], dat.at[r], recv_d.at[r]).wait()
            pltpu.make_async_copy(u.at[r], u.at[r], send_u.at[r]).wait()

    for r in range(FOLD):
        for part in range(2):
            value = dat[r, part]
            for half, row in ((0, r), (1, ROWS - 1 - r)):
                datum[part, pl.ds((row // 8) * 32 + row % 8, 4, stride=8), :] = value[4 * half : 4 * half + 4]

    @pl.when(m < FOLD)
    def _():
        for k in range(stacks):

            @pl.when(k != m)
            def _():
                pltpu.make_async_copy(ready.at[k], ready.at[k], send_d.at[k]).wait()


def vmem():
    return pl.BlockSpec(memory_space=pltpu.VMEM)


def smem():
    return pl.BlockSpec(memory_space=pltpu.SMEM)


def anywhere():
    return pl.BlockSpec(memory_space=pl.ANY)


def shape(*dims):
    return jax.ShapeDtypeStruct(dims, F32)


def scratch(*dims):
    return pltpu.VMEM(dims, F32)


def tiled(x):
    lead = x.shape[:-2]
    k = len(lead)
    return x.reshape(lead + (TILES, 8, 4, 128)).transpose(tuple(range(k)) + (k, k + 2, k + 1, k + 3))


def local(amplitude, phase, validity, iterations, reference_date):
    dma = pltpu.SemaphoreType.DMA
    zr, zi, wt = pl.pallas_call(
        halo_kernel,
        out_shape=[shape(DATES, EXT, 8, 128), shape(DATES, EXT, 8, 128), shape(EXT, 8, 128)],
        in_specs=[anywhere()] * 3,
        out_specs=[vmem()] * 3,
        scratch_shapes=[
            scratch(DATES, EXT, 8, 128),
            scratch(DATES, EXT, 8, 128),
            pltpu.VMEM((EXT, 8, 128), jnp.int32),
            dma((3,)),
            dma((3, 2)),
            dma((3, 2)),
        ],
        compiler_params=pltpu.CompilerParams(
            collective_id=0, has_side_effects=True, vmem_limit_bytes=16 << 20
        ),
        name="halo",
    )(tiled(amplitude), tiled(phase), tiled(validity))
    linked, comp = pl.pallas_call(
        main_kernel,
        out_shape=[shape(2 * DATES, 4 * ROWS, 128), shape(2, FOLD, 8, 128)],
        in_specs=[smem(), smem(), vmem(), vmem(), vmem()],
        out_specs=[vmem(), vmem()],
        scratch_shapes=[
            scratch(EXT, 8, 128),
            scratch(EXT, 8, 128),
            scratch(DATES, FOLD, 8, 128),
            scratch(FOLD, DATES * DATES, 8, 128),
            scratch(FOLD, DATES * DATES, 8, 128),
            scratch(FOLD, DATES * DATES, 8, 128),
            scratch(DATES * DATES, 8, 128),
            scratch(DATES * DATES, 8, 128),
            scratch(DATES * DATES, 8, 128),
            scratch(DATES, 8, 128),
            scratch(2 * DATES, 8, 128),
        ],
        compiler_params=pltpu.CompilerParams(vmem_limit_bytes=40 << 20),
        name="power",
    )(iterations, reference_date, zr, zi, wt)
    datum = pl.pallas_call(
        link_kernel,
        out_shape=shape(2, 4 * ROWS, 128),
        in_specs=[vmem(), vmem()],
        out_specs=vmem(),
        scratch_shapes=[
            scratch(2, FOLD, 8, 128),
            scratch(2, REACH, 8, 128),
            scratch(2, REACH, 8, 128),
            scratch(16, 2, 8, 128),
            scratch(16, 2, 8, 128),
            scratch(16, 2, 8, 128),
            scratch(16, 2, 8, 128),
            dma((2, 5)),
            dma((16,)),
            dma((16,)),
            dma((16,)),
            dma((16,)),
        ],
        compiler_params=pltpu.CompilerParams(
            collective_id=1, has_side_effects=True, vmem_limit_bytes=16 << 20
        ),
        name="links",
    )(comp, wt)
    lr, li = linked[:DATES], linked[DATES:]
    dr, di = datum[0], datum[1]
    out = jnp.stack([lr * dr - li * di, lr * di + li * dr])
    out = out.reshape(2, DATES, TILES, 4, 8, 128).transpose(0, 1, 2, 4, 3, 5)
    return out.reshape(2, DATES, ROWS, 512)


def solution(mesh):
    return jax.shard_map(
        local,
        mesh=mesh,
        in_specs=(P("tm", "space", None), P("tm", "space", None), P("space", None), P("tm"), P("tm")),
        out_specs=P(None, "tm", "space", None),
        check_vma=False,
    )
```

```python
import jax
import jax.numpy as jnp
from jax import lax
from jax.experimental import pallas as pl
from jax.experimental.pallas import tpu as pltpu
from jax.sharding import PartitionSpec as P

MESH = pl.DeviceIdType.MESH
DATES = 10
REACH = 5
FOLD = 12
EXT = FOLD + 2 * REACH
ROWS = 2 * FOLD
TILES = ROWS // 8
MASKED = 0.125
FLOOR = 0.03
F32 = jnp.float32

SIN = (1.0, -1.0 / 6, 1.0 / 120, -1.0 / 5040, 1.0 / 362880, -1.0 / 39916800)
COS = (1.0, -1.0 / 2, 1.0 / 24, -1.0 / 720, 1.0 / 40320, -1.0 / 3628800, 1.0 / 479001600)


def horner(terms, x):
    total = terms[-1] * x + terms[-2]
    for term in terms[-3::-1]:
        total = total * x + term
    return total


def phasor(amplitude, phase):
    half = 0.5 * phase
    square = half * half
    sine = horner(SIN, square) * half
    cosine = horner(COS, square)
    twice = sine + sine
    return amplitude - amplitude * (twice * sine), amplitude * (twice * cosine)


def sublanes():
    return lax.broadcasted_iota(jnp.int32, (8, 128), 0)


def lanes():
    return lax.broadcasted_iota(jnp.int32, (8, 128), 1)


def column_sum():
    lane, block = lanes(), sublanes() & 3
    not_first = jnp.where(block > 0, 1.0, 0.0).astype(F32)
    not_last = jnp.where(block < 3, 1.0, 0.0).astype(F32)
    edges = [(amount, lane >= 128 - amount, lane < amount) for amount in (1, 2)]

    def apply(x):
        before = pltpu.roll(x, 1, 0) * not_first
        after = pltpu.roll(x, 7, 0) * not_last
        total = x
        for amount, high, low in edges:
            total = total + pltpu.roll(jnp.where(high, before, x), amount, 1)
            total = total + pltpu.roll(jnp.where(low, after, x), 128 - amount, 1)
        return total

    return apply


def band_matrix():
    k = lax.broadcasted_iota(jnp.int32, (256, 256), 0) & 127
    n = lax.broadcasted_iota(jnp.int32, (256, 256), 1)
    to = n & 127
    own = (n < 128) & (jnp.abs(k - to) <= 2)
    to_next = (n >= 128) & (to < 64) & (k - 128 >= to - 2)
    to_previous = (n >= 128) & (to >= 64) & (k + 128 <= to + 2)
    return jnp.where(own | to_next | to_previous, 1.0, 0.0).astype(jnp.bfloat16)


def column_sums(band, spill):
    lane, block = lanes(), sublanes() & 3
    from_previous = (lane < 64) & (block > 0)
    from_next = (lane >= 64) & (block < 3)

    def apply(values, slot):
        x = jnp.concatenate(values, axis=0)
        lead = x.astype(jnp.bfloat16)
        rest = (x - lead.astype(F32)).astype(jnp.bfloat16)
        sums = jnp.dot(jnp.concatenate([lead, rest], axis=1), band[...], preferred_element_type=F32)
        spill[slot, pl.ds(8, 8 * len(values))] = sums[:, 128:]
        out = []
        for k in range(len(values)):
            total = sums[8 * k : 8 * k + 8, :128]
            total = total + jnp.where(from_previous, spill[slot, pl.ds(8 * k + 7, 8)], 0.0)
            total = total + jnp.where(from_next, spill[slot, pl.ds(8 * k + 9, 8)], 0.0)
            out.append(total)
        return out

    return apply


def row_sums(values):
    tails = [None] * 11
    tails[10] = values[10]
    for r in range(9, -1, -1):
        tails[r] = tails[r + 1] + values[r]
    out = [tails[0]]
    head = values[11]
    for r in range(1, 11):
        out.append(tails[r] + head)
        head = head + values[r + 11]
    out.append(head)
    return out


def halo_kernel(amp, pha, val, zr, zi, wt, A, B, V, local, send, recv):
    count = lax.axis_size("space")
    me = lax.axis_index("space")
    up, down = lax.rem(me + count - 1, count), lax.rem(me + 1, count)
    arrays = ((amp, A), (pha, B), (val, V))

    def lead(source):
        return (slice(None),) * (len(source.shape) - 4)

    for k, (source, target) in enumerate(arrays):
        all_ = lead(source)
        for r in range(FOLD + REACH):
            for half, row in ((0, r), (1, ROWS - 1 - r)):
                pltpu.make_async_copy(
                    source.at[all_ + (row // 8, slice(None), row % 8)],
                    target.at[all_ + (REACH + r, pl.ds(4 * half, 4))],
                    local.at[k],
                ).start()

    barrier = pltpu.get_barrier_semaphore()
    for neighbour in (up, down):
        pl.semaphore_signal(barrier, inc=1, device_id={"space": neighbour}, device_id_type=MESH)
    pl.semaphore_wait(barrier, 2)

    for k, (source, target) in enumerate(arrays):
        all_ = lead(source)
        for r in range(REACH):
            for half, row, to in ((0, ROWS - 1 - r, down), (1, r, up)):
                pltpu.make_async_remote_copy(
                    source.at[all_ + (row // 8, slice(None), row % 8)],
                    target.at[all_ + (REACH - 1 - r, pl.ds(4 * half, 4))],
                    send.at[k, half],
                    recv.at[k, half],
                    device_id={"space": to},
                    device_id_type=MESH,
                ).start()

    for k, (source, target) in enumerate(arrays):
        own = target.at[lead(source) + (pl.ds(REACH, FOLD + REACH),)]
        pltpu.make_async_copy(own, own, local.at[k]).wait()

    def phasors(first, last):
        def one(d, carry):
            for p in range(first, last):
                real, imag = phasor(A[d, p], B[d, p])
                zr[d, p] = real
                zi[d, p] = imag
            return carry

        lax.fori_loop(0, DATES, one, 0)

    phasors(REACH, EXT)
    for p in range(REACH, EXT):
        wt[p] = jnp.where(V[p] == 1, 1.0, MASKED).astype(F32)

    for k, (source, target) in enumerate(arrays):
        for half in range(2):
            edge = target.at[lead(source) + (pl.ds(0, REACH), pl.ds(4 * half, 4))]
            pltpu.make_async_copy(edge, edge, send.at[k, half]).wait()
            pltpu.make_async_copy(edge, edge, recv.at[k, half]).wait()

    phasors(0, REACH)
    above = jnp.where(me > 0, 1.0, 0.0).astype(F32)
    below = jnp.where(me < count - 1, 1.0, 0.0).astype(F32)
    inside = jnp.where(sublanes() < 4, above, below)
    for p in range(REACH):
        wt[p] = jnp.where(V[p] == 1, 1.0, MASKED).astype(F32) * inside


def main_kernel(iterations, chosen, zr, zi, wt, linked, comp, wr, wi, inv, R, I, S, QR, QI, QS, QD, vec, band, spill):
    band[...] = band_matrix()
    columns = column_sums(band, spill)

    def own_power(k, carry):
        for t in range(2):
            d = 2 * k + t
            values = [wt[p] * (zr[d, p] * zr[d, p] + zi[d, p] * zi[d, p]) for p in range(EXT)]
            for r, total in enumerate(columns(row_sums(values), t)):
                inv[d, r] = 0.5 * lax.rsqrt(total)
        return carry

    lax.fori_loop(0, DATES // 2, own_power, 0)

    def weighted(d, carry):
        for p in range(EXT):
            wr[d, p] = wt[p] * zr[d, p]
            wi[d, p] = wt[p] * zi[d, p]
        return carry

    lax.fori_loop(0, DATES, weighted, 0)

    def matching(turn, carry):
        for t in range(DATES // 2):
            first = lax.rem(turn + t, DATES - 1)
            second = lax.rem(turn + (DATES - 1 - t), DATES - 1) if t else DATES - 1
            i, j = jnp.minimum(first, second), jnp.maximum(first, second)
            real, imag = [], []
            for p in range(EXT):
                a, b, c, d = wr[i, p], wi[i, p], zr[j, p], zi[j, p]
                real.append(a * c + b * d)
                imag.append(b * c - a * d)
            sums = columns(row_sums(real) + row_sums(imag), t)
            for r in range(FOLD):
                scale = inv[i, r] * inv[j, r]
                x = sums[r] * scale
                y = sums[FOLD + r] * scale
                R[r, i * DATES + j] = x
                I[r, i * DATES + j] = y
                S[r, i * DATES + j] = x + y
                S[r, j * DATES + i] = x - y
        return carry

    lax.fori_loop(0, DATES - 1, matching, 0)

    n = iterations[0]
    odd = (n & 1) == 1
    turns = (n - 1) >> 1
    ref = chosen[0]

    def flat(i, j):
        return i * DATES + j

    def upper(i, j):
        return flat(min(i, j), max(i, j))

    def row_total(real, imag, diagonal):
        out_r, out_i = [], []
        for i in range(DATES):
            tr, ti = diagonal(i), None
            for j in range(DATES):
                if j == i:
                    continue
                tr = tr + real(upper(i, j))
                value = imag(upper(i, j))
                if ti is None:
                    ti = value if i < j else -value
                else:
                    ti = ti + value if i < j else ti - value
            out_r.append(tr)
            out_i.append(ti)
        return out_r, out_i

    def position(r, carry):
        squares = [jnp.full((8, 128), 0.25, F32) for _ in range(DATES)]
        for i in range(DATES):
            for j in range(i + 1, DATES):
                k = flat(i, j)
                x, y = R[r, k], I[r, k]
                size = x * x + y * y
                squares[i] = squares[i] + size
                squares[j] = squares[j] + size
        for i in range(DATES):
            QD[i] = squares[i]
        for i in range(DATES):
            for j in range(i + 1, DATES):
                rr, ii, mixed = None, None, None
                for k in range(DATES):
                    if k == i or k == j:
                        continue
                    a = R[r, upper(i, k)] * R[r, upper(j, k)]
                    b = I[r, upper(i, k)] * I[r, upper(j, k)]
                    c = S[r, flat(i, k)] * S[r, flat(k, j)]
                    same = (i < k) == (j < k)
                    rr = a if rr is None else rr + a
                    if ii is None:
                        ii = b if same else -b
                    else:
                        ii = ii + b if same else ii - b
                    mixed = c if mixed is None else mixed + c
                k = flat(i, j)
                x = R[r, k] + (rr + ii)
                y = I[r, k] + (mixed - (rr - ii))
                QR[k] = x
                QI[k] = y
                QS[k] = x + y
                QS[flat(j, i)] = x - y

        one_r, one_i = row_total(lambda k: R[r, k], lambda k: I[r, k], lambda i: jnp.full((8, 128), 0.5, F32))
        two_r, two_i = row_total(lambda k: QR[k], lambda k: QI[k], lambda i: QD[i])
        start = [jnp.where(odd, a, b) for a, b in zip(one_r + one_i, two_r + two_i)]

        def turn(_, v):
            vr, vi = v[:DATES], v[DATES:]
            both = [a + b for a, b in zip(vr, vi)]
            out_r, out_i = [], []
            for i in range(DATES):
                d = QD[i]
                rr, ii, mixed = None, None, None
                for j in range(DATES):
                    if j == i:
                        continue
                    a = QR[upper(i, j)] * vr[j]
                    b = QI[upper(i, j)] * vi[j]
                    c = QS[flat(i, j)] * both[j]
                    rr = a if rr is None else rr + a
                    if ii is None:
                        ii = b if i < j else -b
                    else:
                        ii = ii + b if i < j else ii - b
                    mixed = c if mixed is None else mixed + c
                out_r.append(d * vr[i] + (rr - ii))
                out_i.append(d * vi[i] + (mixed - (rr + ii)))
            return out_r + out_i

        v = lax.fori_loop(0, turns, turn, start)
        total = None
        for x in v:
            total = x * x if total is None else total + x * x
        scale = lax.rsqrt(total)
        v = [x * scale for x in v]
        vr, vi = v[:DATES], v[DATES:]
        for t in range(2 * DATES):
            vec[t] = v[t]
        cr, ci = None, None
        for t in range(DATES):
            a, b = zr[t, r + REACH], zi[t, r + REACH]
            x = vr[t] * a + vi[t] * b
            y = vr[t] * b - vi[t] * a
            cr = x if cr is None else cr + x
            ci = y if ci is None else ci + y
        comp[0, r] = cr
        comp[1, r] = ci
        ref_r, ref_i = DATES * vec[ref], DATES * vec[DATES + ref]
        for t in range(DATES):
            x = vr[t] * ref_r + vi[t] * ref_i
            y = vi[t] * ref_r - vr[t] * ref_i
            for part, value in ((t, x), (DATES + t, y)):
                for half, row in ((0, r), (1, ROWS - 1 - r)):
                    first = (row >> 3) * 32 + (row & 7)
                    linked[part, pl.ds(first, 4, stride=8), :] = value[4 * half : 4 * half + 4]
        return carry

    lax.fori_loop(0, FOLD, position, 0)


def link_kernel(comp, wt, datum, near, own_edge, near_edge, u, got, ready, dat, sem, send_u, recv_u, send_d, recv_d):
    stacks, spaces = lax.axis_size("tm"), lax.axis_size("space")
    m, s = lax.axis_index("tm"), lax.axis_index("space")
    before, after = lax.rem(m + stacks - 1, stacks), lax.rem(m + 1, stacks)
    up, down = lax.rem(s + spaces - 1, spaces), lax.rem(s + 1, spaces)

    barrier = pltpu.get_barrier_semaphore()

    def greet(tm, space):
        pl.semaphore_signal(barrier, inc=1, device_id={"tm": tm, "space": space}, device_id_type=MESH)

    for step in range(1, stacks):
        greet(lax.rem(m + step, stacks), s)
    for space in (up, down):
        greet(m, space)
        greet(before, space)
        greet(after, space)
    pl.semaphore_wait(barrier, stacks - 1 + 6)

    heads, tails = pl.ds(0, 4), pl.ds(4, 4)
    edge = pl.ds(0, REACH)
    plan = (
        (comp, near, (before, s)),
        (comp.at[:, edge, tails], own_edge.at[:, :, heads], (m, down)),
        (comp.at[:, edge, heads], own_edge.at[:, :, tails], (m, up)),
        (comp.at[:, edge, tails], near_edge.at[:, :, heads], (before, down)),
        (comp.at[:, edge, heads], near_edge.at[:, :, tails], (before, up)),
    )
    copies = []
    for k, (source, target, (tm, space)) in enumerate(plan):
        copy = pltpu.make_async_remote_copy(
            source, target, sem.at[0, k], sem.at[1, k], device_id={"tm": tm, "space": space}, device_id_type=MESH
        )
        copy.start()
        copies.append(copy)
    for copy in copies:
        copy.wait()

    def extended(block, edges, part):
        rows = [edges[part, REACH - 1 - k] for k in range(REACH)]
        rows += [block[part, r] for r in range(FOLD)]
        rows += [pltpu.roll(block[part, FOLD - 1 - k], 4, 0) for k in range(REACH)]
        return rows

    ar, ai = extended(comp, own_edge, 0), extended(comp, own_edge, 1)
    br, bi = extended(near, near_edge, 0), extended(near, near_edge, 1)
    columns = column_sum()
    cross_r, cross_i, power_a, power_b = [], [], [], []
    for p in range(EXT):
        w = wt[p]
        xr, xi = w * ar[p], w * ai[p]
        cross_r.append(xr * br[p] + xi * bi[p])
        cross_i.append(xi * br[p] - xr * bi[p])
        power_a.append(xr * ar[p] + xi * ai[p])
        power_b.append(w * (br[p] * br[p] + bi[p] * bi[p]))
    cross_r, cross_i, power_a, power_b = [row_sums(x) for x in (cross_r, cross_i, power_a, power_b)]
    for r in range(FOLD):
        scale = lax.rsqrt((columns(power_a[r]) + 1.0) * (columns(power_b[r]) + 1.0))
        x, y = columns(cross_r[r]) * scale, columns(cross_i[r]) * scale
        bounded = lax.rsqrt(jnp.maximum(x * x + y * y, FLOOR * FLOOR))
        u[r, 0] = x * bounded
        u[r, 1] = y * bounded

    def u_copy(step):
        to = lax.rem(m + step, stacks)
        return to, pltpu.make_async_remote_copy(
            u.at[to], got.at[m], send_u.at[to], recv_u.at[m], device_id={"tm": to}, device_id_type=MESH
        )

    for step in range(1, stacks):
        to = lax.rem(m + step, stacks)

        @pl.when(to < FOLD)
        def _():
            u_copy(step)[1].start()

    @pl.when(m < FOLD)
    def _():
        got[m] = u[m]
        xr, xi = jnp.ones((8, 128), F32), jnp.zeros((8, 128), F32)
        for k in range(stacks):
            ready[k, 0] = xr
            ready[k, 1] = xi

            @pl.when(k != m)
            def _():
                pltpu.make_async_remote_copy(
                    ready.at[k], dat.at[m], send_d.at[k], recv_d.at[m], device_id={"tm": k}, device_id_type=MESH
                ).start()

            @pl.when(k != m)
            def _():
                pltpu.make_async_copy(got.at[k], got.at[k], recv_u.at[k]).wait()

            lr, li = got[k, 0], got[k, 1]
            xr, xi = xr * lr - xi * li, xr * li + xi * lr
        dat[m] = ready[m]

    for r in range(FOLD):

        @pl.when(r != m)
        def _():
            pltpu.make_async_copy(dat.at[r], dat.at[r], recv_d.at[r]).wait()
            pltpu.make_async_copy(u.at[r], u.at[r], send_u.at[r]).wait()

    for r in range(FOLD):
        for part in range(2):
            value = dat[r, part]
            for half, row in ((0, r), (1, ROWS - 1 - r)):
                datum[part, pl.ds((row // 8) * 32 + row % 8, 4, stride=8), :] = value[4 * half : 4 * half + 4]

    @pl.when(m < FOLD)
    def _():
        for k in range(stacks):

            @pl.when(k != m)
            def _():
                pltpu.make_async_copy(ready.at[k], ready.at[k], send_d.at[k]).wait()


def vmem():
    return pl.BlockSpec(memory_space=pltpu.VMEM)


def smem():
    return pl.BlockSpec(memory_space=pltpu.SMEM)


def hbm():
    return pl.BlockSpec(memory_space=pltpu.HBM)


def shape(*dims):
    return jax.ShapeDtypeStruct(dims, F32)


def scratch(*dims):
    return pltpu.VMEM(dims, F32)


def tiled(x):
    lead = x.shape[:-2]
    k = len(lead)
    return x.reshape(lead + (TILES, 8, 4, 128)).transpose(tuple(range(k)) + (k, k + 2, k + 1, k + 3))


def local(amplitude, phase, validity, iterations, reference_date):
    dma = pltpu.SemaphoreType.DMA
    zr, zi, wt = pl.pallas_call(
        halo_kernel,
        out_shape=[shape(DATES, EXT, 8, 128), shape(DATES, EXT, 8, 128), shape(EXT, 8, 128)],
        in_specs=[hbm()] * 3,
        out_specs=[vmem()] * 3,
        scratch_shapes=[
            scratch(DATES, EXT, 8, 128),
            scratch(DATES, EXT, 8, 128),
            pltpu.VMEM((EXT, 8, 128), jnp.int32),
            dma((3,)),
            dma((3, 2)),
            dma((3, 2)),
        ],
        compiler_params=pltpu.CompilerParams(
            collective_id=0, has_side_effects=True, vmem_limit_bytes=16 << 20
        ),
        name="halo",
    )(tiled(amplitude), tiled(phase), tiled(validity))
    linked, comp = pl.pallas_call(
        main_kernel,
        out_shape=[shape(2 * DATES, 4 * ROWS, 128), shape(2, FOLD, 8, 128)],
        in_specs=[smem(), smem(), vmem(), vmem(), vmem()],
        out_specs=[vmem(), vmem()],
        scratch_shapes=[
            scratch(DATES, EXT, 8, 128),
            scratch(DATES, EXT, 8, 128),
            scratch(DATES, FOLD, 8, 128),
            scratch(FOLD, DATES * DATES, 8, 128),
            scratch(FOLD, DATES * DATES, 8, 128),
            scratch(FOLD, DATES * DATES, 8, 128),
            scratch(DATES * DATES, 8, 128),
            scratch(DATES * DATES, 8, 128),
            scratch(DATES * DATES, 8, 128),
            scratch(DATES, 8, 128),
            scratch(2 * DATES, 8, 128),
            pltpu.VMEM((256, 256), jnp.bfloat16),
            scratch(DATES // 2, 16 * FOLD + 16, 128),
        ],
        compiler_params=pltpu.CompilerParams(vmem_limit_bytes=40 << 20),
        name="power",
    )(iterations, reference_date, zr, zi, wt)
    datum = pl.pallas_call(
        link_kernel,
        out_shape=shape(2, 4 * ROWS, 128),
        in_specs=[vmem(), vmem()],
        out_specs=vmem(),
        scratch_shapes=[
            scratch(2, FOLD, 8, 128),
            scratch(2, REACH, 8, 128),
            scratch(2, REACH, 8, 128),
            scratch(16, 2, 8, 128),
            scratch(16, 2, 8, 128),
            scratch(16, 2, 8, 128),
            scratch(16, 2, 8, 128),
            dma((2, 5)),
            dma((16,)),
            dma((16,)),
            dma((16,)),
            dma((16,)),
        ],
        compiler_params=pltpu.CompilerParams(
            collective_id=1, has_side_effects=True, vmem_limit_bytes=16 << 20
        ),
        name="links",
    )(comp, wt)
    lr, li = linked[:DATES], linked[DATES:]
    dr, di = datum[0], datum[1]
    out = jnp.stack([lr * dr - li * di, lr * di + li * dr])
    out = out.reshape(2, DATES, TILES, 4, 8, 128).transpose(0, 1, 2, 4, 3, 5)
    return out.reshape(2, DATES, ROWS, 512)


def solution(mesh):
    return jax.shard_map(
        local,
        mesh=mesh,
        in_specs=(P("tm", "space", None), P("tm", "space", None), P("space", None), P("tm"), P("tm")),
        out_specs=P(None, "tm", "space", None),
        check_vma=False,
    )
```

```python
import jax
import jax.numpy as jnp
from jax import lax
from jax.experimental import pallas as pl
from jax.experimental.pallas import tpu as pltpu
from jax.sharding import PartitionSpec as P

MESH = pl.DeviceIdType.MESH
DATES = 10
REACH = 5
FOLD = 12
EXT = FOLD + 2 * REACH
ROWS = 2 * FOLD
TILES = ROWS // 8
MASKED = 0.125
FLOOR = 0.03
LEAST_TURNS = (10 - 1) // 2
MOST_TURNS = (20 - 1) // 2
THIRD = 40
STAGES = ((4, ((0, 5), (19, 5))), (8, ((5, 4), (15, 4))), (11, ((9, 6),)))
F32 = jnp.float32

SIN = (1.0, -1.0 / 6, 1.0 / 120, -1.0 / 5040, 1.0 / 362880, -1.0 / 39916800)
COS = (1.0, -1.0 / 2, 1.0 / 24, -1.0 / 720, 1.0 / 40320, -1.0 / 3628800, 1.0 / 479001600)


def horner(terms, x):
    total = terms[-1] * x + terms[-2]
    for term in terms[-3::-1]:
        total = total * x + term
    return total


def phasor(amplitude, phase):
    half = 0.5 * phase
    square = half * half
    sine = horner(SIN, square) * half
    cosine = horner(COS, square)
    twice = sine + sine
    return amplitude - amplitude * (twice * sine), amplitude * (twice * cosine)


def sublanes():
    return lax.broadcasted_iota(jnp.int32, (8, 128), 0)


def lanes():
    return lax.broadcasted_iota(jnp.int32, (8, 128), 1)


def column_windows():
    lane, block = lanes(), sublanes() & 3
    not_first = jnp.where(block > 0, 1.0, 0.0).astype(F32)
    not_last = jnp.where(block < 3, 1.0, 0.0).astype(F32)

    def apply(x, y):
        out = []
        for q in range(4):
            pair = (x, y)
            if q == 0:
                pair = [jnp.where(lane >= 126, pltpu.roll(v, 1, 0) * not_first, v) for v in pair]
            if q == 3:
                pair = [jnp.where(lane < 2, pltpu.roll(v, 7, 0) * not_last, v) for v in pair]
            first, second = pair
            start = 2 - 32 * q
            window = jnp.where(lane < THIRD, pltpu.roll(first, start % 128, 1), pltpu.roll(second, (start + THIRD) % 128, 1))
            out.append(jnp.where(lane < 2 * THIRD, window, pltpu.roll(first, (start + 2 * THIRD) % 128, 1)))
        return out

    return apply


def band_matrix():
    k = lax.broadcasted_iota(jnp.int32, (256, 256), 0) & 127
    n = lax.broadcasted_iota(jnp.int32, (256, 256), 1)
    to = n & 127
    own = (n < 128) & (jnp.abs(k - to) <= 2)
    to_next = (n >= 128) & (to < 64) & (k - 128 >= to - 2)
    to_previous = (n >= 128) & (to >= 64) & (k + 128 <= to + 2)
    return jnp.where(own | to_next | to_previous, 1.0, 0.0).astype(jnp.bfloat16)


def column_sums(band, spill):
    lane, block = lanes(), sublanes() & 3
    from_previous = (lane < 64) & (block > 0)
    from_next = (lane >= 64) & (block < 3)

    def apply(values, slot):
        x = jnp.concatenate(values, axis=0)
        lead = x.astype(jnp.bfloat16)
        rest = (x - lead.astype(F32)).astype(jnp.bfloat16)
        sums = jnp.dot(jnp.concatenate([lead, rest], axis=1), band[...], preferred_element_type=F32)
        spill[slot, pl.ds(8, 8 * len(values))] = sums[:, 128:]
        out = []
        for k in range(len(values)):
            total = sums[8 * k : 8 * k + 8, :128]
            total = total + jnp.where(from_previous, spill[slot, pl.ds(8 * k + 7, 8)], 0.0)
            total = total + jnp.where(from_next, spill[slot, pl.ds(8 * k + 9, 8)], 0.0)
            out.append(total)
        return out

    return apply


def row_sums(values):
    tails = [None] * 11
    tails[10] = values[10]
    for r in range(9, -1, -1):
        tails[r] = tails[r + 1] + values[r]
    out = [tails[0]]
    head = values[11]
    for r in range(1, 11):
        out.append(tails[r] + head)
        head = head + values[r + 11]
    out.append(head)
    return out


def long_row_sums(values):
    count = len(values)
    heads, tails = list(values), list(values)
    for p in range(count):
        if p % 11:
            heads[p] = heads[p - 1] + values[p]
    for p in range(count - 2, -1, -1):
        if p % 11 != 10:
            tails[p] = tails[p + 1] + values[p]
    return [tails[r] if r % 11 == 0 else tails[r] + heads[r + 10] for r in range(count - 10)]


def halo_kernel(amp, pha, val, zr, zi, wt, A, B, V, local, send, recv):
    count = lax.axis_size("space")
    me = lax.axis_index("space")
    up, down = lax.rem(me + count - 1, count), lax.rem(me + 1, count)
    arrays = ((amp, A), (pha, B), (val, V))

    def lead(source):
        return (slice(None),) * (len(source.shape) - 4)

    for k, (source, target) in enumerate(arrays):
        all_ = lead(source)
        for r in range(FOLD + REACH):
            for half, row in ((0, r), (1, ROWS - 1 - r)):
                pltpu.make_async_copy(
                    source.at[all_ + (row // 8, slice(None), row % 8)],
                    target.at[all_ + (REACH + r, pl.ds(4 * half, 4))],
                    local.at[k],
                ).start()

    barrier = pltpu.get_barrier_semaphore()
    for neighbour in (up, down):
        pl.semaphore_signal(barrier, inc=1, device_id={"space": neighbour}, device_id_type=MESH)
    pl.semaphore_wait(barrier, 2)

    for k, (source, target) in enumerate(arrays):
        all_ = lead(source)
        for r in range(REACH):
            for half, row, to in ((0, ROWS - 1 - r, down), (1, r, up)):
                pltpu.make_async_remote_copy(
                    source.at[all_ + (row // 8, slice(None), row % 8)],
                    target.at[all_ + (REACH - 1 - r, pl.ds(4 * half, 4))],
                    send.at[k, half],
                    recv.at[k, half],
                    device_id={"space": to},
                    device_id_type=MESH,
                ).start()

    for k, (source, target) in enumerate(arrays):
        own = target.at[lead(source) + (pl.ds(REACH, FOLD + REACH),)]
        pltpu.make_async_copy(own, own, local.at[k]).wait()

    def phasors(first, last):
        def one(d, carry):
            for p in range(first, last):
                real, imag = phasor(A[d, p], B[d, p])
                zr[d, p] = real
                zi[d, p] = imag
            return carry

        lax.fori_loop(0, DATES, one, 0)

    phasors(REACH, EXT)
    for p in range(REACH, EXT):
        wt[p] = jnp.where(V[p] == 1, 1.0, MASKED).astype(F32)

    for k, (source, target) in enumerate(arrays):
        for half in range(2):
            edge = target.at[lead(source) + (pl.ds(0, REACH), pl.ds(4 * half, 4))]
            pltpu.make_async_copy(edge, edge, send.at[k, half]).wait()
            pltpu.make_async_copy(edge, edge, recv.at[k, half]).wait()

    phasors(0, REACH)
    above = jnp.where(me > 0, 1.0, 0.0).astype(F32)
    below = jnp.where(me < count - 1, 1.0, 0.0).astype(F32)
    inside = jnp.where(sublanes() < 4, above, below)
    for p in range(REACH):
        wt[p] = jnp.where(V[p] == 1, 1.0, MASKED).astype(F32) * inside


def main_kernel(
    iterations, chosen, zr, zi, wt, linked, datum,
    wr, wi, inv, R, I, S, QR, QI, QS, QD, vec, band, spill,
    cut, weight, strips, links, parts, whole, send, recv, own, back_send, back_recv,
):
    stacks, spaces = lax.axis_size("tm"), lax.axis_size("space")
    m, s = lax.axis_index("tm"), lax.axis_index("space")
    up, down = lax.rem(s + spaces - 1, spaces), lax.rem(s + 1, spaces)
    barrier = pltpu.get_barrier_semaphore()

    def greet(k, carry):
        for space in (up, s, down):

            @pl.when((k != m) | (space != s))
            def _():
                pl.semaphore_signal(barrier, inc=1, device_id={"tm": k, "space": space}, device_id_type=MESH)

        return carry

    lax.fori_loop(0, stacks, greet, 0)

    band[...] = band_matrix()
    columns = column_sums(band, spill)

    def own_power(k, carry):
        for t in range(2):
            d = 2 * k + t
            values = [wt[p] * (zr[d, p] * zr[d, p] + zi[d, p] * zi[d, p]) for p in range(EXT)]
            for r, total in enumerate(columns(row_sums(values), t)):
                inv[d, r] = 0.5 * lax.rsqrt(total)
        return carry

    lax.fori_loop(0, DATES // 2, own_power, 0)

    def weighted(d, carry):
        for p in range(EXT):
            wr[d, p] = wt[p] * zr[d, p]
            wi[d, p] = wt[p] * zi[d, p]
        return carry

    lax.fori_loop(0, DATES, weighted, 0)

    def matching(turn, carry):
        for t in range(DATES // 2):
            first = lax.rem(turn + t, DATES - 1)
            second = lax.rem(turn + (DATES - 1 - t), DATES - 1) if t else DATES - 1
            i, j = jnp.minimum(first, second), jnp.maximum(first, second)
            real, imag = [], []
            for p in range(EXT):
                a, b, c, d = wr[i, p], wi[i, p], zr[j, p], zi[j, p]
                real.append(a * c + b * d)
                imag.append(b * c - a * d)
            sums = columns(row_sums(real) + row_sums(imag), t)
            for r in range(FOLD):
                scale = inv[i, r] * inv[j, r]
                x = sums[r] * scale
                y = sums[FOLD + r] * scale
                R[r, i * DATES + j] = x
                I[r, i * DATES + j] = y
                S[r, i * DATES + j] = x + y
                S[r, j * DATES + i] = x - y
        return carry

    lax.fori_loop(0, DATES - 1, matching, 0)

    windows = column_windows()
    for p in range(REACH + FOLD):
        for q, window in enumerate(windows(wt[p], wt[p])):
            weight[p, 4 * q : 4 * q + 4] = window[:4]
            weight[ROWS + 2 * REACH - 1 - p, 4 * q : 4 * q + 4] = window[4:]

    pl.semaphore_wait(barrier, 3 * stacks - 1)

    n = iterations[0]
    odd = (n & 1) == 1
    turns = (n - 1) >> 1
    ref = chosen[0]

    def flat(i, j):
        return i * DATES + j

    def upper(i, j):
        return flat(min(i, j), max(i, j))

    def row_total(real, imag, diagonal):
        out_r, out_i = [], []
        for i in range(DATES):
            tr, ti = diagonal(i), None
            for j in range(DATES):
                if j == i:
                    continue
                tr = tr + real(upper(i, j))
                value = imag(upper(i, j))
                if ti is None:
                    ti = value if i < j else -value
                else:
                    ti = ti + value if i < j else ti - value
            out_r.append(tr)
            out_i.append(ti)
        return out_r, out_i

    def position(r, carry):
        squares = [jnp.full((8, 128), 0.25, F32) for _ in range(DATES)]
        for i in range(DATES):
            for j in range(i + 1, DATES):
                k = flat(i, j)
                x, y = R[r, k], I[r, k]
                size = x * x + y * y
                squares[i] = squares[i] + size
                squares[j] = squares[j] + size
        for i in range(DATES):
            QD[i] = squares[i]
        for i in range(DATES):
            for j in range(i + 1, DATES):
                rr, ii, mixed = None, None, None
                for k in range(DATES):
                    if k == i or k == j:
                        continue
                    a = R[r, upper(i, k)] * R[r, upper(j, k)]
                    b = I[r, upper(i, k)] * I[r, upper(j, k)]
                    c = S[r, flat(i, k)] * S[r, flat(k, j)]
                    same = (i < k) == (j < k)
                    rr = a if rr is None else rr + a
                    if ii is None:
                        ii = b if same else -b
                    else:
                        ii = ii + b if same else ii - b
                    mixed = c if mixed is None else mixed + c
                k = flat(i, j)
                x = R[r, k] + (rr + ii)
                y = I[r, k] + (mixed - (rr - ii))
                QR[k] = x
                QI[k] = y
                QS[k] = x + y
                QS[flat(j, i)] = x - y

        one_r, one_i = row_total(lambda k: R[r, k], lambda k: I[r, k], lambda i: jnp.full((8, 128), 0.5, F32))
        two_r, two_i = row_total(lambda k: QR[k], lambda k: QI[k], lambda i: QD[i])
        start = [jnp.where(odd, a, b) for a, b in zip(one_r + one_i, two_r + two_i)]

        def turn(count, v):
            vr, vi = v[:DATES], v[DATES:]
            both = [a + b for a, b in zip(vr, vi)]
            out_r, out_i = [], []
            for i in range(DATES):
                d = QD[i]
                rr, ii, mixed = None, None, None
                for j in range(DATES):
                    if j == i:
                        continue
                    a = QR[upper(i, j)] * vr[j]
                    b = QI[upper(i, j)] * vi[j]
                    c = QS[flat(i, j)] * both[j]
                    rr = a if rr is None else rr + a
                    if ii is None:
                        ii = b if i < j else -b
                    else:
                        ii = ii + b if i < j else ii - b
                    mixed = c if mixed is None else mixed + c
                out_r.append(d * vr[i] + (rr - ii))
                out_i.append(d * vi[i] + (mixed - (rr + ii)))
            return out_r + out_i

        def maybe(count, v):
            return [jnp.where(count < turns, a, b) for a, b in zip(turn(count, v), v)]

        v = lax.fori_loop(0, LEAST_TURNS, turn, start)
        v = lax.fori_loop(LEAST_TURNS, MOST_TURNS, maybe, v)
        total = None
        for x in v:
            total = x * x if total is None else total + x * x
        scale = lax.rsqrt(total)
        v = [x * scale for x in v]
        vr, vi = v[:DATES], v[DATES:]
        for t in range(2 * DATES):
            vec[t] = v[t]
        cr, ci = None, None
        for t in range(DATES):
            a, b = zr[t, r + REACH], zi[t, r + REACH]
            x = vr[t] * a + vi[t] * b
            y = vr[t] * b - vi[t] * a
            cr = x if cr is None else cr + x
            ci = y if ci is None else ci + y
        for q, window in enumerate(windows(cr, ci)):
            cut[r, 4 * q : 4 * q + 4] = window[:4]
            cut[ROWS - 1 - r, 4 * q : 4 * q + 4] = window[4:]
        ref_r, ref_i = DATES * vec[ref], DATES * vec[DATES + ref]
        for t in range(DATES):
            x = vr[t] * ref_r + vi[t] * ref_i
            y = vi[t] * ref_r - vr[t] * ref_i
            for part, value in ((t, x), (DATES + t, y)):
                for half, row in ((0, r), (1, ROWS - 1 - r)):
                    first = (row >> 3) * 32 + (row & 7)
                    linked[part, pl.ds(first, 4, stride=8), :] = value[4 * half : 4 * half + 4]
        for last, pieces in STAGES:

            @pl.when(r == last)
            def _():
                lax.fori_loop(0, stacks, lambda k, c: share(k, c, pieces), 0)

        return carry

    def share(k, carry, pieces):
        def start(first, size, to, space):
            pltpu.make_async_remote_copy(
                cut.at[pl.ds(first, size), k],
                strips.at[pl.ds(to, size), m],
                send,
                recv,
                device_id={"tm": k, "space": space},
                device_id_type=MESH,
            ).start()

        for first, size in pieces:

            @pl.when(k != m)
            def _():
                start(first, size, REACH + first, s)

            if first == 0:
                start(first, REACH, REACH + ROWS, up)
            if first + size == ROWS:
                start(first + size - REACH, REACH, 0, down)
        return carry

    lax.fori_loop(0, FOLD, position, 0)

    mine = pltpu.make_async_copy(cut.at[:, m], strips.at[pl.ds(REACH, ROWS), m], own)
    mine.start()
    mine.wait()
    everything = strips.at[:, pl.ds(0, 13)]
    pltpu.make_async_copy(everything, everything, recv).wait()
    lane, sub = lanes(), sublanes()
    halves = (pl.ds(0, 8), pl.ds(8, 8))

    def next_stack(pair):
        second = pltpu.roll(pair[1], 7, 0)
        return jnp.where(sub < 7, pltpu.roll(pair[0], 7, 0), second), second

    low, middle = lane < THIRD, lane < 2 * THIRD
    fields = ([], [])
    for p in range(ROWS + 2 * REACH):
        w = jnp.broadcast_to(weight[p, pl.ds(m, 1)], (8, 128))
        pair = [strips[p, half] for half in halves]
        for field, x, y in zip(fields, pair, next_stack(pair)):
            straight = x * y
            crossed = x * pltpu.roll(y, 128 - THIRD, 1)
            power = x * x
            value = jnp.where(
                low,
                straight + pltpu.roll(straight, 128 - THIRD, 1),
                jnp.where(
                    middle, crossed - pltpu.roll(crossed, THIRD, 1), power + pltpu.roll(power, THIRD, 1)
                ),
            )
            field.append(w * value)
    sums = [long_row_sums(field) for field in fields]
    for r in range(ROWS):
        pair = []
        for half in range(2):
            x = sums[half][r]
            for amount in (1, 2, 127, 126):
                x = x + pltpu.roll(sums[half][r], amount, 1)
            pair.append(x)
        for half, x, y in zip(halves, pair, next_stack(pair)):
            scale = lax.rsqrt((x + 1.0) * (y + 1.0))
            x = x * jnp.where(low, pltpu.roll(scale, 128 - 2 * THIRD, 1), pltpu.roll(scale, 128 - THIRD, 1))
            size = x * x
            size = size + jnp.where(low, pltpu.roll(size, 128 - THIRD, 1), pltpu.roll(size, THIRD, 1))
            first = 16 * r + (half.start)
            links[pl.ds(first, 8)] = x * lax.rsqrt(jnp.maximum(size, FLOOR * FLOOR))

    xr = [jnp.ones((8, 128), F32)] * TILES
    xi = [jnp.zeros((8, 128), F32)] * TILES
    for k in range(stacks):
        for t in range(TILES):
            parts[k, 8 * t : 8 * t + 8] = jnp.where(low, xr[t], pltpu.roll(xi[t], THIRD, 1))

        @pl.when(k != m)
        def _():
            pltpu.make_async_remote_copy(
                parts.at[k], whole.at[m], back_send, back_recv, device_id={"tm": k}, device_id_type=MESH
            ).start()

        if k < stacks - 1:
            for t in range(TILES):
                lr = links[pl.ds(128 * t + k, 8, stride=16)]
                li = pltpu.roll(lr, 128 - THIRD, 1)
                xr[t], xi[t] = xr[t] * lr - xi[t] * li, xr[t] * li + xi[t] * lr
    whole[m] = parts[m]
    most = whole.at[pl.ds(0, stacks - 1)]
    pltpu.make_async_copy(most, most, back_recv).wait()

    for t in range(TILES):
        for b in range(4):
            real, imag = None, None
            for q in range(4):
                x = whole[4 * q + b, 8 * t : 8 * t + 8]
                a = pltpu.roll(x, (32 * q - 2) % 128, 1)
                c = pltpu.roll(x, (32 * q - 2 - THIRD) % 128, 1)
                real = a if q == 0 else jnp.where(lane < 32 * q, real, a)
                imag = c if q == 0 else jnp.where(lane < 32 * q, imag, c)
            datum[0, 8 * (4 * t + b) : 8 * (4 * t + b) + 8] = real
            datum[1, 8 * (4 * t + b) : 8 * (4 * t + b) + 8] = imag
    pltpu.make_async_copy(everything, everything, send).wait()
    pltpu.make_async_copy(most, most, back_send).wait()


def vmem():
    return pl.BlockSpec(memory_space=pltpu.VMEM)


def smem():
    return pl.BlockSpec(memory_space=pltpu.SMEM)


def hbm():
    return pl.BlockSpec(memory_space=pltpu.HBM)


def shape(*dims):
    return jax.ShapeDtypeStruct(dims, F32)


def scratch(*dims):
    return pltpu.VMEM(dims, F32)


def tiled(x):
    lead = x.shape[:-2]
    k = len(lead)
    return x.reshape(lead + (TILES, 8, 4, 128)).transpose(tuple(range(k)) + (k, k + 2, k + 1, k + 3))


def local(amplitude, phase, validity, iterations, reference_date):
    dma = pltpu.SemaphoreType.DMA
    zr, zi, wt = pl.pallas_call(
        halo_kernel,
        out_shape=[shape(DATES, EXT, 8, 128), shape(DATES, EXT, 8, 128), shape(EXT, 8, 128)],
        in_specs=[hbm()] * 3,
        out_specs=[vmem()] * 3,
        scratch_shapes=[
            scratch(DATES, EXT, 8, 128),
            scratch(DATES, EXT, 8, 128),
            pltpu.VMEM((EXT, 8, 128), jnp.int32),
            dma((3,)),
            dma((3, 2)),
            dma((3, 2)),
        ],
        compiler_params=pltpu.CompilerParams(
            collective_id=0, has_side_effects=True, vmem_limit_bytes=16 << 20
        ),
        name="halo",
    )(tiled(amplitude), tiled(phase), tiled(validity))
    linked, datum = pl.pallas_call(
        main_kernel,
        out_shape=[shape(2 * DATES, 4 * ROWS, 128), shape(2, 4 * ROWS, 128)],
        in_specs=[smem(), smem(), vmem(), vmem(), vmem()],
        out_specs=[vmem(), vmem()],
        scratch_shapes=[
            scratch(DATES, EXT, 8, 128),
            scratch(DATES, EXT, 8, 128),
            scratch(DATES, FOLD, 8, 128),
            scratch(FOLD, DATES * DATES, 8, 128),
            scratch(FOLD, DATES * DATES, 8, 128),
            scratch(FOLD, DATES * DATES, 8, 128),
            scratch(DATES * DATES, 8, 128),
            scratch(DATES * DATES, 8, 128),
            scratch(DATES * DATES, 8, 128),
            scratch(DATES, 8, 128),
            scratch(2 * DATES, 8, 128),
            pltpu.VMEM((256, 256), jnp.bfloat16),
            scratch(DATES // 2, 16 * FOLD + 16, 128),
            scratch(ROWS, 16, 128),
            scratch(ROWS + 2 * REACH, 16, 128),
            scratch(40, 16, 128),
            scratch(16 * ROWS, 128),
            scratch(16, ROWS, 128),
            scratch(16, ROWS, 128),
            dma(()),
            dma(()),
            dma(()),
            dma(()),
            dma(()),
        ],
        compiler_params=pltpu.CompilerParams(
            collective_id=1, has_side_effects=True, vmem_limit_bytes=40 << 20
        ),
        name="power",
    )(iterations, reference_date, zr, zi, wt)
    lr, li = linked[:DATES], linked[DATES:]
    dr, di = datum[0], datum[1]
    out = jnp.stack([lr * dr - li * di, lr * di + li * dr])
    out = out.reshape(2, DATES, TILES, 4, 8, 128).transpose(0, 1, 2, 4, 3, 5)
    return out.reshape(2, DATES, ROWS, 512)


def solution(mesh):
    return jax.shard_map(
        local,
        mesh=mesh,
        in_specs=(P("tm", "space", None), P("tm", "space", None), P("space", None), P("tm"), P("tm")),
        out_specs=P(None, "tm", "space", None),
        check_vma=False,
    )
```

```python
import jax
import jax.numpy as jnp
from jax import lax
from jax.experimental import pallas as pl
from jax.experimental.pallas import tpu as pltpu
from jax.sharding import PartitionSpec as P

MESH = pl.DeviceIdType.MESH
DATES = 10
REACH = 5
FOLD = 12
EXT = FOLD + 2 * REACH
ROWS = 2 * FOLD
TILES = ROWS // 8
MASKED = 0.125
FLOOR = 0.03
LEAST_TURNS = (10 - 1) // 2
MOST_TURNS = (20 - 1) // 2
THIRD = 40
STAGES = ((4, ((0, 5), (19, 5))), (8, ((5, 4), (15, 4))), (11, ((9, 6),)))
F32 = jnp.float32

SIN = (1.0, -1.0 / 6, 1.0 / 120, -1.0 / 5040, 1.0 / 362880, -1.0 / 39916800)
COS = (1.0, -1.0 / 2, 1.0 / 24, -1.0 / 720, 1.0 / 40320, -1.0 / 3628800, 1.0 / 479001600)


def horner(terms, x):
    total = terms[-1] * x + terms[-2]
    for term in terms[-3::-1]:
        total = total * x + term
    return total


def phasor(amplitude, phase):
    half = 0.5 * phase
    square = half * half
    sine = horner(SIN, square) * half
    cosine = horner(COS, square)
    twice = sine + sine
    return amplitude - amplitude * (twice * sine), amplitude * (twice * cosine)


def sublanes():
    return lax.broadcasted_iota(jnp.int32, (8, 128), 0)


def lanes():
    return lax.broadcasted_iota(jnp.int32, (8, 128), 1)


def column_windows():
    lane, block = lanes(), sublanes() & 3
    not_first = jnp.where(block > 0, 1.0, 0.0).astype(F32)
    not_last = jnp.where(block < 3, 1.0, 0.0).astype(F32)

    def apply(x, y):
        out = []
        for q in range(4):
            pair = (x, y)
            if q == 0:
                pair = [jnp.where(lane >= 126, pltpu.roll(v, 1, 0) * not_first, v) for v in pair]
            if q == 3:
                pair = [jnp.where(lane < 2, pltpu.roll(v, 7, 0) * not_last, v) for v in pair]
            first, second = pair
            start = 2 - 32 * q
            window = jnp.where(lane < THIRD, pltpu.roll(first, start % 128, 1), pltpu.roll(second, (start + THIRD) % 128, 1))
            out.append(jnp.where(lane < 2 * THIRD, window, pltpu.roll(first, (start + 2 * THIRD) % 128, 1)))
        return out

    return apply


def band_matrix():
    k = lax.broadcasted_iota(jnp.int32, (256, 256), 0) & 127
    n = lax.broadcasted_iota(jnp.int32, (256, 256), 1)
    to = n & 127
    own = (n < 128) & (jnp.abs(k - to) <= 2)
    to_next = (n >= 128) & (to < 64) & (k - 128 >= to - 2)
    to_previous = (n >= 128) & (to >= 64) & (k + 128 <= to + 2)
    return jnp.where(own | to_next | to_previous, 1.0, 0.0).astype(jnp.bfloat16)


def column_sums(band, spill):
    lane, block = lanes(), sublanes() & 3
    from_previous = (lane < 64) & (block > 0)
    from_next = (lane >= 64) & (block < 3)

    def apply(values, slot):
        x = jnp.concatenate(values, axis=0)
        lead = x.astype(jnp.bfloat16)
        rest = (x - lead.astype(F32)).astype(jnp.bfloat16)
        sums = jnp.dot(jnp.concatenate([lead, rest], axis=1), band[...], preferred_element_type=F32)
        spill[slot, pl.ds(8, 8 * len(values))] = sums[:, 128:]
        out = []
        for k in range(len(values)):
            total = sums[8 * k : 8 * k + 8, :128]
            total = total + jnp.where(from_previous, spill[slot, pl.ds(8 * k + 7, 8)], 0.0)
            total = total + jnp.where(from_next, spill[slot, pl.ds(8 * k + 9, 8)], 0.0)
            out.append(total)
        return out

    return apply


def row_sums(values):
    tails = [None] * 11
    tails[10] = values[10]
    for r in range(9, -1, -1):
        tails[r] = tails[r + 1] + values[r]
    out = [tails[0]]
    head = values[11]
    for r in range(1, 11):
        out.append(tails[r] + head)
        head = head + values[r + 11]
    out.append(head)
    return out


def long_row_sums(values):
    count = len(values)
    heads, tails = list(values), list(values)
    for p in range(count):
        if p % 11:
            heads[p] = heads[p - 1] + values[p]
    for p in range(count - 2, -1, -1):
        if p % 11 != 10:
            tails[p] = tails[p + 1] + values[p]
    return [tails[r] if r % 11 == 0 else tails[r] + heads[r + 10] for r in range(count - 10)]


def halo_kernel(amp, pha, val, zr, zi, wt, A, B, V, local, send, recv):
    count = lax.axis_size("space")
    me = lax.axis_index("space")
    up, down = lax.rem(me + count - 1, count), lax.rem(me + 1, count)
    arrays = ((amp, A), (pha, B), (val, V))

    def lead(source):
        return (slice(None),) * (len(source.shape) - 4)

    barrier = pltpu.get_barrier_semaphore()
    for neighbour in (up, down):
        pl.semaphore_signal(barrier, inc=1, device_id={"space": neighbour}, device_id_type=MESH)
    for k, (source, target) in enumerate(arrays):
        all_ = lead(source)
        for r in range(FOLD + REACH):
            for half, row in ((0, r), (1, ROWS - 1 - r)):
                pltpu.make_async_copy(
                    source.at[all_ + (row // 8, slice(None), row % 8)],
                    target.at[all_ + (REACH + r, pl.ds(4 * half, 4))],
                    local.at[k],
                ).start()

    pl.semaphore_wait(barrier, 2)

    for k, (source, target) in enumerate(arrays):
        all_ = lead(source)
        for r in range(REACH):
            for half, row, to in ((0, ROWS - 1 - r, down), (1, r, up)):
                pltpu.make_async_remote_copy(
                    source.at[all_ + (row // 8, slice(None), row % 8)],
                    target.at[all_ + (REACH - 1 - r, pl.ds(4 * half, 4))],
                    send.at[k, half],
                    recv.at[k, half],
                    device_id={"space": to},
                    device_id_type=MESH,
                ).start()

    for k, (source, target) in enumerate(arrays):
        own = target.at[lead(source) + (pl.ds(REACH, FOLD + REACH),)]
        pltpu.make_async_copy(own, own, local.at[k]).wait()

    def phasors(first, last):
        def one(d, carry):
            for p in range(first, last):
                real, imag = phasor(A[d, p], B[d, p])
                zr[d, p] = real
                zi[d, p] = imag
            return carry

        lax.fori_loop(0, DATES, one, 0)

    phasors(REACH, EXT)
    for p in range(REACH, EXT):
        wt[p] = jnp.where(V[p] == 1, 1.0, MASKED).astype(F32)

    for k, (source, target) in enumerate(arrays):
        for half in range(2):
            edge = target.at[lead(source) + (pl.ds(0, REACH), pl.ds(4 * half, 4))]
            pltpu.make_async_copy(edge, edge, send.at[k, half]).wait()
            pltpu.make_async_copy(edge, edge, recv.at[k, half]).wait()

    phasors(0, REACH)
    above = jnp.where(me > 0, 1.0, 0.0).astype(F32)
    below = jnp.where(me < count - 1, 1.0, 0.0).astype(F32)
    inside = jnp.where(sublanes() < 4, above, below)
    for p in range(REACH):
        wt[p] = jnp.where(V[p] == 1, 1.0, MASKED).astype(F32) * inside


def main_kernel(
    iterations, chosen, zr, zi, wt, linked_r, linked_i, datum, turned_datum,
    wr, wi, inv, R, I, S, QR, QI, QS, QD, vec, band, spill,
    cut, weight, far_weight, strips, links, parts, whole, send, recv, own, back_send, back_recv,
):
    stacks, spaces = lax.axis_size("tm"), lax.axis_size("space")
    m, s = lax.axis_index("tm"), lax.axis_index("space")
    partner = lax.rem(s + spaces // 2, spaces)
    up, down = lax.rem(partner + spaces - 1, spaces), lax.rem(partner + 1, spaces)
    barrier = pltpu.get_barrier_semaphore()

    def greet(k, carry):
        for space in (up, partner, down):
            pl.semaphore_signal(barrier, inc=1, device_id={"tm": k, "space": space}, device_id_type=MESH)
        return carry

    lax.fori_loop(0, stacks, greet, 0)

    band[...] = band_matrix()
    columns = column_sums(band, spill)

    def own_power(k, carry):
        for t in range(2):
            d = 2 * k + t
            values = [wt[p] * (zr[d, p] * zr[d, p] + zi[d, p] * zi[d, p]) for p in range(EXT)]
            for r, total in enumerate(columns(row_sums(values), t)):
                inv[d, r] = 0.5 * lax.rsqrt(total)
        return carry

    lax.fori_loop(0, DATES // 2, own_power, 0)

    def weighted(d, carry):
        for p in range(EXT):
            wr[d, p] = wt[p] * zr[d, p]
            wi[d, p] = wt[p] * zi[d, p]
        return carry

    lax.fori_loop(0, DATES, weighted, 0)

    def matching(turn, carry):
        for t in range(DATES // 2):
            first = lax.rem(turn + t, DATES - 1)
            second = lax.rem(turn + (DATES - 1 - t), DATES - 1) if t else DATES - 1
            i, j = jnp.minimum(first, second), jnp.maximum(first, second)
            real, imag = [], []
            for p in range(EXT):
                a, b, c, d = wr[i, p], wi[i, p], zr[j, p], zi[j, p]
                real.append(a * c + b * d)
                imag.append(b * c - a * d)
            sums = columns(row_sums(real) + row_sums(imag), t)
            for r in range(FOLD):
                scale = inv[i, r] * inv[j, r]
                x = sums[r] * scale
                y = sums[FOLD + r] * scale
                R[r, i * DATES + j] = x
                I[r, i * DATES + j] = y
                S[r, i * DATES + j] = x + y
                S[r, j * DATES + i] = x - y
        return carry

    lax.fori_loop(0, DATES - 1, matching, 0)

    windows = column_windows()
    for p in range(REACH + FOLD):
        for q, window in enumerate(windows(wt[p], wt[p])):
            weight[p, 4 * q : 4 * q + 4] = window[:4]
            weight[ROWS + 2 * REACH - 1 - p, 4 * q : 4 * q + 4] = window[4:]

    pl.semaphore_wait(barrier, 3 * stacks)
    weights = pltpu.make_async_remote_copy(
        weight.at[:, m], far_weight, *own, device_id={"space": partner}, device_id_type=MESH
    )
    weights.start()

    n = iterations[0]
    odd = (n & 1) == 1
    turns = (n - 1) >> 1
    ref = chosen[0]

    def flat(i, j):
        return i * DATES + j

    def upper(i, j):
        return flat(min(i, j), max(i, j))

    def row_total(real, imag, diagonal):
        out_r, out_i = [], []
        for i in range(DATES):
            tr, ti = diagonal(i), None
            for j in range(DATES):
                if j == i:
                    continue
                tr = tr + real(upper(i, j))
                value = imag(upper(i, j))
                if ti is None:
                    ti = value if i < j else -value
                else:
                    ti = ti + value if i < j else ti - value
            out_r.append(tr)
            out_i.append(ti)
        return out_r, out_i

    def position(r, carry):
        squares = [jnp.full((8, 128), 0.25, F32) for _ in range(DATES)]
        for i in range(DATES):
            for j in range(i + 1, DATES):
                k = flat(i, j)
                x, y = R[r, k], I[r, k]
                size = x * x + y * y
                squares[i] = squares[i] + size
                squares[j] = squares[j] + size
        for i in range(DATES):
            QD[i] = squares[i]
        for i in range(DATES):
            for j in range(i + 1, DATES):
                rr, ii, mixed = None, None, None
                for k in range(DATES):
                    if k == i or k == j:
                        continue
                    a = R[r, upper(i, k)] * R[r, upper(j, k)]
                    b = I[r, upper(i, k)] * I[r, upper(j, k)]
                    c = S[r, flat(i, k)] * S[r, flat(k, j)]
                    same = (i < k) == (j < k)
                    rr = a if rr is None else rr + a
                    if ii is None:
                        ii = b if same else -b
                    else:
                        ii = ii + b if same else ii - b
                    mixed = c if mixed is None else mixed + c
                k = flat(i, j)
                x = R[r, k] + (rr + ii)
                y = I[r, k] + (mixed - (rr - ii))
                QR[k] = x
                QI[k] = y
                QS[k] = x + y
                QS[flat(j, i)] = x - y

        one_r, one_i = row_total(lambda k: R[r, k], lambda k: I[r, k], lambda i: jnp.full((8, 128), 0.5, F32))
        two_r, two_i = row_total(lambda k: QR[k], lambda k: QI[k], lambda i: QD[i])
        start = [jnp.where(odd, a, b) for a, b in zip(one_r + one_i, two_r + two_i)]

        def turn(count, v):
            vr, vi = v[:DATES], v[DATES:]
            both = [a + b for a, b in zip(vr, vi)]
            out_r, out_i = [], []
            for i in range(DATES):
                d = QD[i]
                rr, ii, mixed = None, None, None
                for j in range(DATES):
                    if j == i:
                        continue
                    a = QR[upper(i, j)] * vr[j]
                    b = QI[upper(i, j)] * vi[j]
                    c = QS[flat(i, j)] * both[j]
                    rr = a if rr is None else rr + a
                    if ii is None:
                        ii = b if i < j else -b
                    else:
                        ii = ii + b if i < j else ii - b
                    mixed = c if mixed is None else mixed + c
                out_r.append(d * vr[i] + (rr - ii))
                out_i.append(d * vi[i] + (mixed - (rr + ii)))
            return out_r + out_i

        def maybe(count, v):
            return [jnp.where(count < turns, a, b) for a, b in zip(turn(count, v), v)]

        v = lax.fori_loop(0, LEAST_TURNS, turn, start)
        v = lax.fori_loop(LEAST_TURNS, MOST_TURNS, maybe, v)
        total = None
        for x in v:
            total = x * x if total is None else total + x * x
        scale = lax.rsqrt(total)
        v = [x * scale for x in v]
        vr, vi = v[:DATES], v[DATES:]
        for t in range(2 * DATES):
            vec[t] = v[t]
        cr, ci = None, None
        for t in range(DATES):
            a, b = zr[t, r + REACH], zi[t, r + REACH]
            x = vr[t] * a + vi[t] * b
            y = vr[t] * b - vi[t] * a
            cr = x if cr is None else cr + x
            ci = y if ci is None else ci + y
        for q, window in enumerate(windows(cr, ci)):
            cut[r, 4 * q : 4 * q + 4] = window[:4]
            cut[ROWS - 1 - r, 4 * q : 4 * q + 4] = window[4:]
        ref_r, ref_i = DATES * vec[ref], DATES * vec[DATES + ref]
        for t in range(DATES):
            x = vr[t] * ref_r + vi[t] * ref_i
            y = vi[t] * ref_r - vr[t] * ref_i
            for target, value in ((linked_r, x), (linked_i, y)):
                for half, row in ((0, r), (1, ROWS - 1 - r)):
                    first = (row >> 3) * 32 + (row & 7)
                    target[t, pl.ds(first, 4, stride=8), :] = value[4 * half : 4 * half + 4]
        for last, pieces in STAGES:

            @pl.when(r == last)
            def _():
                lax.fori_loop(0, stacks, lambda k, c: share(k, c, pieces), 0)

        return carry

    def share(k, carry, pieces):
        def start(first, size, to, space):
            pltpu.make_async_remote_copy(
                cut.at[pl.ds(first, size), k],
                strips.at[pl.ds(to, size), m],
                send,
                recv,
                device_id={"tm": k, "space": space},
                device_id_type=MESH,
            ).start()

        for first, size in pieces:

            start(first, size, REACH + first, partner)
            if first == 0:
                start(first, REACH, REACH + ROWS, up)
            if first + size == ROWS:
                start(first + size - REACH, REACH, 0, down)
        return carry

    lax.fori_loop(0, FOLD, position, 0)

    weights.wait()
    pltpu.make_async_copy(strips, strips, recv).wait()
    lane, sub = lanes(), sublanes()
    halves = (pl.ds(0, 8), pl.ds(8, 8))

    def next_stack(pair):
        second = pltpu.roll(pair[1], 7, 0)
        return jnp.where(sub < 7, pltpu.roll(pair[0], 7, 0), second), second

    low, middle, left = lane < THIRD, lane < 2 * THIRD, lane < 64
    fields = ([], [])
    for p in range(ROWS + 2 * REACH):
        w = jnp.broadcast_to(far_weight[pl.ds(p, 1)], (8, 128))
        pair = [strips[p, half] for half in halves]
        for field, x, y in zip(fields, pair, next_stack(pair)):
            straight = x * y
            crossed = x * pltpu.roll(y, 128 - THIRD, 1)
            power = x * x
            value = jnp.where(
                low,
                straight + pltpu.roll(straight, 128 - THIRD, 1),
                jnp.where(
                    middle, crossed - pltpu.roll(crossed, THIRD, 1), power + pltpu.roll(power, THIRD, 1)
                ),
            )
            field.append(w * value)
    sums = [long_row_sums(field) for field in fields]
    for r in range(ROWS):
        pair = []
        for half in range(2):
            x = sums[half][r]
            for amount in (127, 126, 125, 124):
                x = x + pltpu.roll(sums[half][r], amount, 1)
            pair.append(x)
        for half, x, y in zip(halves, pair, next_stack(pair)):
            scale = lax.rsqrt((x + 1.0) * (y + 1.0))
            x = x * jnp.where(low, pltpu.roll(scale, 128 - 2 * THIRD, 1), pltpu.roll(scale, 128 - THIRD, 1))
            size = x * x
            size = size + jnp.where(low, pltpu.roll(size, 128 - THIRD, 1), pltpu.roll(size, THIRD, 1))
            first = 16 * r + (half.start)
            links[pl.ds(first, 8)] = x * lax.rsqrt(jnp.maximum(size, FLOOR * FLOOR))

    xr = [jnp.ones((8, 128), F32)] * TILES
    xi = [jnp.zeros((8, 128), F32)] * TILES
    for k in range(stacks):
        tiles = [jnp.where(lane < 32, xr[t], pltpu.roll(xi[t], 32, 1)) for t in range(TILES)]
        parts[k, 0:8] = jnp.where(left, tiles[0], pltpu.roll(tiles[1], 64, 1))
        parts[k, 8:16] = jnp.where(left, tiles[2], pltpu.roll(pltpu.roll(tiles[2], 64, 1), 4, 0))
        pltpu.make_async_remote_copy(
            parts.at[k, pl.ds(0, 12)],
            whole.at[m, pl.ds(0, 12)],
            back_send,
            back_recv,
            device_id={"tm": k, "space": partner},
            device_id_type=MESH,
        ).start()
        if k < stacks - 1:
            for t in range(TILES):
                lr = links[pl.ds(128 * t + k, 8, stride=16)]
                li = pltpu.roll(lr, 128 - THIRD, 1)
                xr[t], xi[t] = xr[t] * lr - xi[t] * li, xr[t] * li + xi[t] * lr
    most = whole.at[:, pl.ds(0, 12)]
    pltpu.make_async_copy(most, most, back_recv).wait()

    for b in range(4):
        joined = [None] * 6
        for q in range(4):
            x, y = whole[4 * q + b, 0:8], whole[4 * q + b, 8:16]
            y = jnp.where(sub < 4, y, pltpu.roll(pltpu.roll(y, 64, 1), 4, 0))
            for n in range(6):
                source, quarter = (x, n) if n < 4 else (y, n - 4)
                amount = 32 * (q - quarter) % 128
                turned = pltpu.roll(source, amount, 1) if amount else source
                joined[n] = turned if q == 0 else jnp.where(lane < 32 * q, joined[n], turned)
        for t in range(TILES):
            rows = pl.ds(8 * (4 * t + b), 8)
            datum[0, rows] = joined[2 * t]
            datum[1, rows] = joined[2 * t + 1]
            turned_datum[0, rows] = -joined[2 * t + 1]
            turned_datum[1, rows] = joined[2 * t]
    pltpu.make_async_copy(strips, strips, send).wait()
    pltpu.make_async_copy(most, most, back_send).wait()


def vmem():
    return pl.BlockSpec(memory_space=pltpu.VMEM)


def smem():
    return pl.BlockSpec(memory_space=pltpu.SMEM)


def hbm():
    return pl.BlockSpec(memory_space=pltpu.HBM)


def shape(*dims):
    return jax.ShapeDtypeStruct(dims, F32)


def scratch(*dims):
    return pltpu.VMEM(dims, F32)


def tiled(x):
    lead = x.shape[:-2]
    k = len(lead)
    return x.reshape(lead + (TILES, 8, 4, 128)).transpose(tuple(range(k)) + (k, k + 2, k + 1, k + 3))


def local(amplitude, phase, validity, iterations, reference_date):
    dma = pltpu.SemaphoreType.DMA
    zr, zi, wt = pl.pallas_call(
        halo_kernel,
        out_shape=[shape(DATES, EXT, 8, 128), shape(DATES, EXT, 8, 128), shape(EXT, 8, 128)],
        in_specs=[hbm()] * 3,
        out_specs=[vmem()] * 3,
        scratch_shapes=[
            scratch(DATES, EXT, 8, 128),
            scratch(DATES, EXT, 8, 128),
            pltpu.VMEM((EXT, 8, 128), jnp.int32),
            dma((3,)),
            dma((3, 2)),
            dma((3, 2)),
        ],
        compiler_params=pltpu.CompilerParams(
            collective_id=0, has_side_effects=True, vmem_limit_bytes=16 << 20
        ),
        name="halo",
    )(*[pltpu.with_memory_space_constraint(tiled(x), pltpu.HBM) for x in (amplitude, phase, validity)])
    linked_r, linked_i, datum, turned = pl.pallas_call(
        main_kernel,
        out_shape=[shape(DATES, 4 * ROWS, 128)] * 2 + [shape(2, 4 * ROWS, 128)] * 2,
        in_specs=[smem(), smem(), vmem(), vmem(), vmem()],
        out_specs=[vmem()] * 4,
        scratch_shapes=[
            scratch(DATES, EXT, 8, 128),
            scratch(DATES, EXT, 8, 128),
            scratch(DATES, FOLD, 8, 128),
            scratch(FOLD, DATES * DATES, 8, 128),
            scratch(FOLD, DATES * DATES, 8, 128),
            scratch(FOLD, DATES * DATES, 8, 128),
            scratch(DATES * DATES, 8, 128),
            scratch(DATES * DATES, 8, 128),
            scratch(DATES * DATES, 8, 128),
            scratch(DATES, 8, 128),
            scratch(2 * DATES, 8, 128),
            pltpu.VMEM((256, 256), jnp.bfloat16),
            scratch(DATES // 2, 16 * FOLD + 16, 128),
            scratch(ROWS, 16, 128),
            scratch(ROWS + 2 * REACH, 16, 128),
            scratch(ROWS + 2 * REACH, 128),
            scratch(ROWS + 2 * REACH, 16, 128),
            scratch(16 * ROWS, 128),
            scratch(16, 16, 128),
            scratch(16, 16, 128),
            dma(()),
            dma(()),
            [dma(()), dma(())],
            dma(()),
            dma(()),
        ],
        compiler_params=pltpu.CompilerParams(
            collective_id=1, has_side_effects=True, vmem_limit_bytes=40 << 20
        ),
        name="power",
    )(iterations, reference_date, zr, zi, wt)
    out = linked_r * datum[:, None] + linked_i * turned[:, None]
    out = out.reshape(2, DATES, TILES, 4, 8, 128).transpose(0, 1, 2, 4, 3, 5)
    return out.reshape(2, DATES, ROWS, 512)


def solution(mesh):
    return jax.shard_map(
        local,
        mesh=mesh,
        in_specs=(P("tm", "space", None), P("tm", "space", None), P("space", None), P("tm"), P("tm")),
        out_specs=P(None, "tm", "space", None),
        check_vma=False,
    )
```

```python
import jax
import jax.numpy as jnp
from jax import lax
from jax.experimental import pallas as pl
from jax.experimental.pallas import tpu as pltpu
from jax.sharding import PartitionSpec as P

MESH = pl.DeviceIdType.MESH
DATES = 10
REACH = 5
FOLD = 12
EXT = FOLD + 2 * REACH
ROWS = 2 * FOLD
TILES = ROWS // 8
MASKED = 0.125
FLOOR = 0.03
LEAST_TURNS = (10 - 1) // 2
MOST_TURNS = (20 - 1) // 2
THIRD = 40
STAGES = ((4, ()), (8, ((0, 9), (15, 9))), (11, ((9, 6),)))
F32 = jnp.float32

SIN = (1.0, -1.0 / 6, 1.0 / 120, -1.0 / 5040, 1.0 / 362880, -1.0 / 39916800)
COS = (1.0, -1.0 / 2, 1.0 / 24, -1.0 / 720, 1.0 / 40320, -1.0 / 3628800, 1.0 / 479001600)


def horner(terms, x):
    total = terms[-1] * x + terms[-2]
    for term in terms[-3::-1]:
        total = total * x + term
    return total


def phasor(amplitude, phase):
    half = 0.5 * phase
    square = half * half
    sine = horner(SIN, square) * half
    cosine = horner(COS, square)
    twice = sine + sine
    return amplitude - amplitude * (twice * sine), amplitude * (twice * cosine)


def sublanes():
    return lax.broadcasted_iota(jnp.int32, (8, 128), 0)


def lanes():
    return lax.broadcasted_iota(jnp.int32, (8, 128), 1)


def column_windows():
    lane, block = lanes(), sublanes() & 3
    not_first = jnp.where(block > 0, 1.0, 0.0).astype(F32)
    not_last = jnp.where(block < 3, 1.0, 0.0).astype(F32)

    def apply(x, y):
        out = []
        for q in range(4):
            pair = (x, y)
            if q == 0:
                pair = [jnp.where(lane >= 126, pltpu.roll(v, 1, 0) * not_first, v) for v in pair]
            if q == 3:
                pair = [jnp.where(lane < 2, pltpu.roll(v, 7, 0) * not_last, v) for v in pair]
            first, second = pair
            start = 2 - 32 * q
            window = jnp.where(lane < THIRD, pltpu.roll(first, start % 128, 1), pltpu.roll(second, (start + THIRD) % 128, 1))
            out.append(jnp.where(lane < 2 * THIRD, window, pltpu.roll(first, (start + 2 * THIRD) % 128, 1)))
        return out

    return apply


def band_matrix():
    k = lax.broadcasted_iota(jnp.int32, (256, 256), 0) & 127
    n = lax.broadcasted_iota(jnp.int32, (256, 256), 1)
    to = n & 127
    own = (n < 128) & (jnp.abs(k - to) <= 2)
    to_next = (n >= 128) & (to < 64) & (k - 128 >= to - 2)
    to_previous = (n >= 128) & (to >= 64) & (k + 128 <= to + 2)
    return jnp.where(own | to_next | to_previous, 1.0, 0.0).astype(jnp.bfloat16)


def column_sums(band, spill):
    lane, block = lanes(), sublanes() & 3
    from_previous = (lane < 64) & (block > 0)
    from_next = (lane >= 64) & (block < 3)

    def apply(values, slot):
        x = jnp.concatenate(values, axis=0)
        lead = x.astype(jnp.bfloat16)
        rest = (x - lead.astype(F32)).astype(jnp.bfloat16)
        sums = jnp.dot(jnp.concatenate([lead, rest], axis=1), band[...], preferred_element_type=F32)
        spill[slot, pl.ds(8, 8 * len(values))] = sums[:, 128:]
        out = []
        for k in range(len(values)):
            total = sums[8 * k : 8 * k + 8, :128]
            total = total + jnp.where(from_previous, spill[slot, pl.ds(8 * k + 7, 8)], 0.0)
            total = total + jnp.where(from_next, spill[slot, pl.ds(8 * k + 9, 8)], 0.0)
            out.append(total)
        return out

    return apply


def row_sums(values):
    tails = [None] * 11
    tails[10] = values[10]
    for r in range(9, -1, -1):
        tails[r] = tails[r + 1] + values[r]
    out = [tails[0]]
    head = values[11]
    for r in range(1, 11):
        out.append(tails[r] + head)
        head = head + values[r + 11]
    out.append(head)
    return out


def long_row_sums(values):
    count = len(values)
    heads, tails = list(values), list(values)
    for p in range(count):
        if p % 11:
            heads[p] = heads[p - 1] + values[p]
    for p in range(count - 2, -1, -1):
        if p % 11 != 10:
            tails[p] = tails[p + 1] + values[p]
    return [tails[r] if r % 11 == 0 else tails[r] + heads[r + 10] for r in range(count - 10)]


def halo_kernel(amp, pha, val, zr, zi, wt, A, B, V, local, send, recv):
    count = lax.axis_size("space")
    me = lax.axis_index("space")
    up, down = lax.rem(me + count - 1, count), lax.rem(me + 1, count)
    arrays = ((amp, A), (pha, B), (val, V))

    def lead(source):
        return (slice(None),) * (len(source.shape) - 4)

    barrier = pltpu.get_barrier_semaphore()
    for neighbour in (up, down):
        pl.semaphore_signal(barrier, inc=1, device_id={"space": neighbour}, device_id_type=MESH)
    for k, (source, target) in enumerate(arrays):
        all_ = lead(source)
        for r in range(FOLD + REACH):
            for half, row in ((0, r), (1, ROWS - 1 - r)):
                pltpu.make_async_copy(
                    source.at[all_ + (row // 8, slice(None), row % 8)],
                    target.at[all_ + (REACH + r, pl.ds(4 * half, 4))],
                    local.at[k],
                ).start()

    pl.semaphore_wait(barrier, 2)

    for k, (source, target) in enumerate(arrays):
        all_ = lead(source)
        for r in range(REACH):
            for half, row, to in ((0, ROWS - 1 - r, down), (1, r, up)):
                pltpu.make_async_remote_copy(
                    source.at[all_ + (row // 8, slice(None), row % 8)],
                    target.at[all_ + (REACH - 1 - r, pl.ds(4 * half, 4))],
                    send.at[k, half],
                    recv.at[k, half],
                    device_id={"space": to},
                    device_id_type=MESH,
                ).start()

    for k, (source, target) in enumerate(arrays):
        own = target.at[lead(source) + (pl.ds(REACH, FOLD + REACH),)]
        pltpu.make_async_copy(own, own, local.at[k]).wait()

    def phasors(first, last):
        def one(d, carry):
            for p in range(first, last):
                real, imag = phasor(A[d, p], B[d, p])
                zr[d, p] = real
                zi[d, p] = imag
            return carry

        lax.fori_loop(0, DATES, one, 0)

    phasors(REACH, EXT)
    for p in range(REACH, EXT):
        wt[p] = jnp.where(V[p] == 1, 1.0, MASKED).astype(F32)

    for k, (source, target) in enumerate(arrays):
        for half in range(2):
            edge = target.at[lead(source) + (pl.ds(0, REACH), pl.ds(4 * half, 4))]
            pltpu.make_async_copy(edge, edge, send.at[k, half]).wait()
            pltpu.make_async_copy(edge, edge, recv.at[k, half]).wait()

    phasors(0, REACH)
    above = jnp.where(me > 0, 1.0, 0.0).astype(F32)
    below = jnp.where(me < count - 1, 1.0, 0.0).astype(F32)
    inside = jnp.where(sublanes() < 4, above, below)
    for p in range(REACH):
        wt[p] = jnp.where(V[p] == 1, 1.0, MASKED).astype(F32) * inside


def main_kernel(
    iterations, chosen, zr, zi, wt, linked_r, linked_i, datum, turned_datum,
    wr, wi, inv, R, I, S, QR, QI, QS, QD, vec, band, spill,
    cut, weight, far_weight, strips, links, parts, whole, send, recv, own, back_send, back_recv,
):
    stacks, spaces = lax.axis_size("tm"), lax.axis_size("space")
    m, s = lax.axis_index("tm"), lax.axis_index("space")
    partner = lax.rem(s + spaces // 2, spaces)
    up, down = lax.rem(partner + spaces - 1, spaces), lax.rem(partner + 1, spaces)
    barrier = pltpu.get_barrier_semaphore()

    def greet(k, carry):
        for space in (up, partner, down):
            pl.semaphore_signal(barrier, inc=1, device_id={"tm": k, "space": space}, device_id_type=MESH)
        return carry

    lax.fori_loop(0, stacks, greet, 0)

    band[...] = band_matrix()
    columns = column_sums(band, spill)

    def own_power(k, carry):
        for t in range(2):
            d = 2 * k + t
            values = [wt[p] * (zr[d, p] * zr[d, p] + zi[d, p] * zi[d, p]) for p in range(EXT)]
            for r, total in enumerate(columns(row_sums(values), t)):
                inv[d, r] = 0.5 * lax.rsqrt(total)
        return carry

    lax.fori_loop(0, DATES // 2, own_power, 0)

    def weighted(d, carry):
        for p in range(EXT):
            wr[d, p] = wt[p] * zr[d, p]
            wi[d, p] = wt[p] * zi[d, p]
        return carry

    lax.fori_loop(0, DATES, weighted, 0)

    def matching(turn, carry):
        for t in range(DATES // 2):
            first = lax.rem(turn + t, DATES - 1)
            second = lax.rem(turn + (DATES - 1 - t), DATES - 1) if t else DATES - 1
            i, j = jnp.minimum(first, second), jnp.maximum(first, second)
            real, imag = [], []
            for p in range(EXT):
                a, b, c, d = wr[i, p], wi[i, p], zr[j, p], zi[j, p]
                real.append(a * c + b * d)
                imag.append(b * c - a * d)
            sums = columns(row_sums(real) + row_sums(imag), t)
            for r in range(FOLD):
                scale = inv[i, r] * inv[j, r]
                x = sums[r] * scale
                y = sums[FOLD + r] * scale
                R[r, i * DATES + j] = x
                I[r, i * DATES + j] = y
                S[r, i * DATES + j] = x + y
                S[r, j * DATES + i] = x - y
        return carry

    lax.fori_loop(0, DATES - 1, matching, 0)

    windows = column_windows()
    for p in range(REACH + FOLD):
        for q, window in enumerate(windows(wt[p], wt[p])):
            weight[p, 4 * q : 4 * q + 4] = window[:4]
            weight[ROWS + 2 * REACH - 1 - p, 4 * q : 4 * q + 4] = window[4:]

    pl.semaphore_wait(barrier, 3 * stacks)
    weights = pltpu.make_async_remote_copy(
        weight.at[:, m], far_weight, *own, device_id={"space": partner}, device_id_type=MESH
    )
    weights.start()

    n = iterations[0]
    odd = (n & 1) == 1
    turns = (n - 1) >> 1
    ref = chosen[0]

    def flat(i, j):
        return i * DATES + j

    def upper(i, j):
        return flat(min(i, j), max(i, j))

    def row_total(real, imag, diagonal):
        out_r, out_i = [], []
        for i in range(DATES):
            tr, ti = diagonal(i), None
            for j in range(DATES):
                if j == i:
                    continue
                tr = tr + real(upper(i, j))
                value = imag(upper(i, j))
                if ti is None:
                    ti = value if i < j else -value
                else:
                    ti = ti + value if i < j else ti - value
            out_r.append(tr)
            out_i.append(ti)
        return out_r, out_i

    def position(r, carry):
        squares = [jnp.full((8, 128), 0.25, F32) for _ in range(DATES)]
        for i in range(DATES):
            for j in range(i + 1, DATES):
                k = flat(i, j)
                x, y = R[r, k], I[r, k]
                size = x * x + y * y
                squares[i] = squares[i] + size
                squares[j] = squares[j] + size
        for i in range(DATES):
            QD[i] = squares[i]
        for i in range(DATES):
            for j in range(i + 1, DATES):
                rr, ii, mixed = None, None, None
                for k in range(DATES):
                    if k == i or k == j:
                        continue
                    a = R[r, upper(i, k)] * R[r, upper(j, k)]
                    b = I[r, upper(i, k)] * I[r, upper(j, k)]
                    c = S[r, flat(i, k)] * S[r, flat(k, j)]
                    same = (i < k) == (j < k)
                    rr = a if rr is None else rr + a
                    if ii is None:
                        ii = b if same else -b
                    else:
                        ii = ii + b if same else ii - b
                    mixed = c if mixed is None else mixed + c
                k = flat(i, j)
                x = R[r, k] + (rr + ii)
                y = I[r, k] + (mixed - (rr - ii))
                QR[k] = x
                QI[k] = y
                QS[k] = x + y
                QS[flat(j, i)] = x - y

        one_r, one_i = row_total(lambda k: R[r, k], lambda k: I[r, k], lambda i: jnp.full((8, 128), 0.5, F32))
        two_r, two_i = row_total(lambda k: QR[k], lambda k: QI[k], lambda i: QD[i])
        start = [jnp.where(odd, a, b) for a, b in zip(one_r + one_i, two_r + two_i)]

        def turn(count, v):
            vr, vi = v[:DATES], v[DATES:]
            both = [a + b for a, b in zip(vr, vi)]
            out_r, out_i = [], []
            for i in range(DATES):
                d = QD[i]
                rr, ii, mixed = None, None, None
                for j in range(DATES):
                    if j == i:
                        continue
                    a = QR[upper(i, j)] * vr[j]
                    b = QI[upper(i, j)] * vi[j]
                    c = QS[flat(i, j)] * both[j]
                    rr = a if rr is None else rr + a
                    if ii is None:
                        ii = b if i < j else -b
                    else:
                        ii = ii + b if i < j else ii - b
                    mixed = c if mixed is None else mixed + c
                out_r.append(d * vr[i] + (rr - ii))
                out_i.append(d * vi[i] + (mixed - (rr + ii)))
            return out_r + out_i

        def maybe(count, v):
            return [jnp.where(count < turns, a, b) for a, b in zip(turn(count, v), v)]

        v = lax.fori_loop(0, LEAST_TURNS, turn, start)
        v = lax.fori_loop(LEAST_TURNS, MOST_TURNS, maybe, v)
        total = None
        for x in v:
            total = x * x if total is None else total + x * x
        scale = lax.rsqrt(total)
        v = [x * scale for x in v]
        vr, vi = v[:DATES], v[DATES:]
        for t in range(2 * DATES):
            vec[t] = v[t]
        cr, ci = None, None
        for t in range(DATES):
            a, b = zr[t, r + REACH], zi[t, r + REACH]
            x = vr[t] * a + vi[t] * b
            y = vr[t] * b - vi[t] * a
            cr = x if cr is None else cr + x
            ci = y if ci is None else ci + y
        for q, window in enumerate(windows(cr, ci)):
            cut[r, 4 * q : 4 * q + 4] = window[:4]
            cut[ROWS - 1 - r, 4 * q : 4 * q + 4] = window[4:]
        ref_r, ref_i = DATES * vec[ref], DATES * vec[DATES + ref]
        for t in range(DATES):
            x = vr[t] * ref_r + vi[t] * ref_i
            y = vi[t] * ref_r - vr[t] * ref_i
            for target, value in ((linked_r, x), (linked_i, y)):
                for half, row in ((0, r), (1, ROWS - 1 - r)):
                    first = (row >> 3) * 32 + (row & 7)
                    target[t, pl.ds(first, 4, stride=8), :] = value[4 * half : 4 * half + 4]
        for last, pieces in STAGES:

            @pl.when(r == last)
            def _():
                lax.fori_loop(0, stacks, lambda k, c: share(k, c, pieces), 0)

        return carry

    def share(k, carry, pieces):
        def start(first, size, to, space):
            pltpu.make_async_remote_copy(
                cut.at[pl.ds(first, size), k],
                strips.at[pl.ds(to, size), m],
                send,
                recv,
                device_id={"tm": k, "space": space},
                device_id_type=MESH,
            ).start()

        for first, size in pieces:

            start(first, size, REACH + first, partner)
        if not pieces:
            start(0, REACH, REACH + ROWS, up)
            start(ROWS - REACH, REACH, 0, down)
        return carry

    lax.fori_loop(0, FOLD, position, 0)

    weights.wait()
    pltpu.make_async_copy(strips, strips, recv).wait()
    lane, sub = lanes(), sublanes()
    halves = (pl.ds(0, 8), pl.ds(8, 8))

    def next_stack(pair):
        second = pltpu.roll(pair[1], 7, 0)
        return jnp.where(sub < 7, pltpu.roll(pair[0], 7, 0), second), second

    low, middle, left = lane < THIRD, lane < 2 * THIRD, lane < 64
    fields = ([], [])
    for p in range(ROWS + 2 * REACH):
        w = jnp.broadcast_to(far_weight[pl.ds(p, 1)], (8, 128))
        pair = [strips[p, half] for half in halves]
        for field, x, y in zip(fields, pair, next_stack(pair)):
            straight = x * y
            crossed = x * pltpu.roll(y, 128 - THIRD, 1)
            power = x * x
            value = jnp.where(
                low,
                straight + pltpu.roll(straight, 128 - THIRD, 1),
                jnp.where(
                    middle, crossed - pltpu.roll(crossed, THIRD, 1), power + pltpu.roll(power, THIRD, 1)
                ),
            )
            field.append(w * value)
    sums = [long_row_sums(field) for field in fields]
    for r in range(ROWS):
        pair = []
        for half in range(2):
            x = sums[half][r]
            for amount in (127, 126, 125, 124):
                x = x + pltpu.roll(sums[half][r], amount, 1)
            pair.append(x)
        for half, x, y in zip(halves, pair, next_stack(pair)):
            scale = lax.rsqrt((x + 1.0) * (y + 1.0))
            x = x * jnp.where(low, pltpu.roll(scale, 128 - 2 * THIRD, 1), pltpu.roll(scale, 128 - THIRD, 1))
            size = x * x
            size = size + jnp.where(low, pltpu.roll(size, 128 - THIRD, 1), pltpu.roll(size, THIRD, 1))
            first = 16 * r + (half.start)
            links[pl.ds(first, 8)] = x * lax.rsqrt(jnp.maximum(size, FLOOR * FLOOR))

    xr = [jnp.ones((8, 128), F32)] * TILES
    xi = [jnp.zeros((8, 128), F32)] * TILES
    for k in range(stacks):
        tiles = [jnp.where(lane < 32, xr[t], pltpu.roll(xi[t], 32, 1)) for t in range(TILES)]
        parts[k, 0:8] = jnp.where(left, tiles[0], pltpu.roll(tiles[1], 64, 1))
        parts[k, 8:16] = jnp.where(left, tiles[2], pltpu.roll(pltpu.roll(tiles[2], 64, 1), 4, 0))
        pltpu.make_async_remote_copy(
            parts.at[k, pl.ds(0, 12)],
            whole.at[m, pl.ds(0, 12)],
            back_send,
            back_recv,
            device_id={"tm": k, "space": partner},
            device_id_type=MESH,
        ).start()
        if k < stacks - 1:
            for t in range(TILES):
                lr = links[pl.ds(128 * t + k, 8, stride=16)]
                li = pltpu.roll(lr, 128 - THIRD, 1)
                xr[t], xi[t] = xr[t] * lr - xi[t] * li, xr[t] * li + xi[t] * lr
    most = whole.at[:, pl.ds(0, 12)]
    pltpu.make_async_copy(most, most, back_recv).wait()

    for b in range(4):
        joined = [None] * 6
        for q in range(4):
            x, y = whole[4 * q + b, 0:8], whole[4 * q + b, 8:16]
            y = jnp.where(sub < 4, y, pltpu.roll(pltpu.roll(y, 64, 1), 4, 0))
            for n in range(6):
                source, quarter = (x, n) if n < 4 else (y, n - 4)
                amount = 32 * (q - quarter) % 128
                turned = pltpu.roll(source, amount, 1) if amount else source
                joined[n] = turned if q == 0 else jnp.where(lane < 32 * q, joined[n], turned)
        for t in range(TILES):
            rows = pl.ds(8 * (4 * t + b), 8)
            datum[0, rows] = joined[2 * t]
            datum[1, rows] = joined[2 * t + 1]
            turned_datum[0, rows] = -joined[2 * t + 1]
            turned_datum[1, rows] = joined[2 * t]
    pltpu.make_async_copy(strips, strips, send).wait()
    pltpu.make_async_copy(most, most, back_send).wait()


def vmem():
    return pl.BlockSpec(memory_space=pltpu.VMEM)


def smem():
    return pl.BlockSpec(memory_space=pltpu.SMEM)


def hbm():
    return pl.BlockSpec(memory_space=pltpu.HBM)


def shape(*dims):
    return jax.ShapeDtypeStruct(dims, F32)


def scratch(*dims):
    return pltpu.VMEM(dims, F32)


def tiled(x):
    lead = x.shape[:-2]
    k = len(lead)
    return x.reshape(lead + (TILES, 8, 4, 128)).transpose(tuple(range(k)) + (k, k + 2, k + 1, k + 3))


def local(amplitude, phase, validity, iterations, reference_date):
    dma = pltpu.SemaphoreType.DMA
    zr, zi, wt = pl.pallas_call(
        halo_kernel,
        out_shape=[shape(DATES, EXT, 8, 128), shape(DATES, EXT, 8, 128), shape(EXT, 8, 128)],
        in_specs=[hbm()] * 3,
        out_specs=[vmem()] * 3,
        scratch_shapes=[
            scratch(DATES, EXT, 8, 128),
            scratch(DATES, EXT, 8, 128),
            pltpu.VMEM((EXT, 8, 128), jnp.int32),
            dma((3,)),
            dma((3, 2)),
            dma((3, 2)),
        ],
        compiler_params=pltpu.CompilerParams(
            collective_id=0, has_side_effects=True, vmem_limit_bytes=16 << 20
        ),
        name="halo",
    )(*[pltpu.with_memory_space_constraint(tiled(x), pltpu.HBM) for x in (amplitude, phase, validity)])
    linked_r, linked_i, datum, turned = pl.pallas_call(
        main_kernel,
        out_shape=[shape(DATES, 4 * ROWS, 128)] * 2 + [shape(2, 4 * ROWS, 128)] * 2,
        in_specs=[smem(), smem(), vmem(), vmem(), vmem()],
        out_specs=[vmem()] * 4,
        scratch_shapes=[
            scratch(DATES, EXT, 8, 128),
            scratch(DATES, EXT, 8, 128),
            scratch(DATES, FOLD, 8, 128),
            scratch(FOLD, DATES * DATES, 8, 128),
            scratch(FOLD, DATES * DATES, 8, 128),
            scratch(FOLD, DATES * DATES, 8, 128),
            scratch(DATES * DATES, 8, 128),
            scratch(DATES * DATES, 8, 128),
            scratch(DATES * DATES, 8, 128),
            scratch(DATES, 8, 128),
            scratch(2 * DATES, 8, 128),
            pltpu.VMEM((256, 256), jnp.bfloat16),
            scratch(DATES // 2, 16 * FOLD + 16, 128),
            scratch(ROWS, 16, 128),
            scratch(ROWS + 2 * REACH, 16, 128),
            scratch(ROWS + 2 * REACH, 128),
            scratch(ROWS + 2 * REACH, 16, 128),
            scratch(16 * ROWS, 128),
            scratch(16, 16, 128),
            scratch(16, 16, 128),
            dma(()),
            dma(()),
            [dma(()), dma(())],
            dma(()),
            dma(()),
        ],
        compiler_params=pltpu.CompilerParams(
            collective_id=1, has_side_effects=True, vmem_limit_bytes=40 << 20
        ),
        name="power",
    )(iterations, reference_date, zr, zi, wt)
    out = linked_r * datum[:, None] + linked_i * turned[:, None]
    out = out.reshape(2, DATES, TILES, 4, 8, 128).transpose(0, 1, 2, 4, 3, 5)
    return out.reshape(2, DATES, ROWS, 512)


def solution(mesh):
    return jax.shard_map(
        local,
        mesh=mesh,
        in_specs=(P("tm", "space", None), P("tm", "space", None), P("space", None), P("tm"), P("tm")),
        out_specs=P(None, "tm", "space", None),
        check_vma=False,
    )
```

```python
import jax
import jax.numpy as jnp
from jax import lax
from jax.experimental import pallas as pl
from jax.experimental.pallas import tpu as pltpu
from jax.sharding import PartitionSpec as P

MESH = pl.DeviceIdType.MESH
DATES = 10
REACH = 5
FOLD = 12
EXT = FOLD + 2 * REACH
ROWS = 2 * FOLD
TILES = ROWS // 8
MASKED = 0.125
FLOOR = 0.03
LEAST_TURNS = (10 - 1) // 2
MOST_TURNS = (20 - 1) // 2
THIRD = 40
STAGES = ((4, ()), (8, ((0, 9), (15, 9))), (11, ((9, 6),)))
F32 = jnp.float32

SIN = (1.0, -1.0 / 6, 1.0 / 120, -1.0 / 5040, 1.0 / 362880, -1.0 / 39916800)
COS = (1.0, -1.0 / 2, 1.0 / 24, -1.0 / 720, 1.0 / 40320, -1.0 / 3628800, 1.0 / 479001600)


def horner(terms, x):
    total = terms[-1] * x + terms[-2]
    for term in terms[-3::-1]:
        total = total * x + term
    return total


def phasor(amplitude, phase):
    half = 0.5 * phase
    square = half * half
    sine = horner(SIN, square) * half
    cosine = horner(COS, square)
    twice = sine + sine
    return amplitude - amplitude * (twice * sine), amplitude * (twice * cosine)


def sublanes():
    return lax.broadcasted_iota(jnp.int32, (8, 128), 0)


def lanes():
    return lax.broadcasted_iota(jnp.int32, (8, 128), 1)


def column_windows():
    lane, block = lanes(), sublanes() & 3
    not_first = jnp.where(block > 0, 1.0, 0.0).astype(F32)
    not_last = jnp.where(block < 3, 1.0, 0.0).astype(F32)

    def apply(x, y):
        out = []
        for q in range(4):
            pair = (x, y)
            if q == 0:
                pair = [jnp.where(lane >= 126, pltpu.roll(v, 1, 0) * not_first, v) for v in pair]
            if q == 3:
                pair = [jnp.where(lane < 2, pltpu.roll(v, 7, 0) * not_last, v) for v in pair]
            first, second = pair
            start = 2 - 32 * q
            window = jnp.where(lane < THIRD, pltpu.roll(first, start % 128, 1), pltpu.roll(second, (start + THIRD) % 128, 1))
            out.append(jnp.where(lane < 2 * THIRD, window, pltpu.roll(first, (start + 2 * THIRD) % 128, 1)))
        return out

    return apply


def band_matrix():
    k = lax.broadcasted_iota(jnp.int32, (256, 256), 0) & 127
    n = lax.broadcasted_iota(jnp.int32, (256, 256), 1)
    to = n & 127
    own = (n < 128) & (jnp.abs(k - to) <= 2)
    to_next = (n >= 128) & (to < 64) & (k - 128 >= to - 2)
    to_previous = (n >= 128) & (to >= 64) & (k + 128 <= to + 2)
    return jnp.where(own | to_next | to_previous, 1.0, 0.0).astype(jnp.bfloat16)


def column_sums(band, spill):
    lane, block = lanes(), sublanes() & 3
    from_previous = (lane < 64) & (block > 0)
    from_next = (lane >= 64) & (block < 3)

    def apply(values, slot):
        x = jnp.concatenate(values, axis=0)
        lead = x.astype(jnp.bfloat16)
        rest = (x - lead.astype(F32)).astype(jnp.bfloat16)
        sums = jnp.dot(jnp.concatenate([lead, rest], axis=1), band[...], preferred_element_type=F32)
        spill[slot, pl.ds(8, 8 * len(values))] = sums[:, 128:]
        out = []
        for k in range(len(values)):
            total = sums[8 * k : 8 * k + 8, :128]
            total = total + jnp.where(from_previous, spill[slot, pl.ds(8 * k + 7, 8)], 0.0)
            total = total + jnp.where(from_next, spill[slot, pl.ds(8 * k + 9, 8)], 0.0)
            out.append(total)
        return out

    return apply


def row_sums(values):
    tails = [None] * 11
    tails[10] = values[10]
    for r in range(9, -1, -1):
        tails[r] = tails[r + 1] + values[r]
    out = [tails[0]]
    head = values[11]
    for r in range(1, 11):
        out.append(tails[r] + head)
        head = head + values[r + 11]
    out.append(head)
    return out


def long_row_sums(values):
    count = len(values)
    heads, tails = list(values), list(values)
    for p in range(count):
        if p % 11:
            heads[p] = heads[p - 1] + values[p]
    for p in range(count - 2, -1, -1):
        if p % 11 != 10:
            tails[p] = tails[p + 1] + values[p]
    return [tails[r] if r % 11 == 0 else tails[r] + heads[r + 10] for r in range(count - 10)]


def halo_kernel(amp, pha, val, zr, zi, wt, A, B, V, local, send, recv):
    count = lax.axis_size("space")
    me = lax.axis_index("space")
    up, down = lax.rem(me + count - 1, count), lax.rem(me + 1, count)
    arrays = ((amp, A), (pha, B), (val, V))

    def lead(source):
        return (slice(None),) * (len(source.shape) - 4)

    barrier = pltpu.get_barrier_semaphore()
    for neighbour in (up, down):
        pl.semaphore_signal(barrier, inc=1, device_id={"space": neighbour}, device_id_type=MESH)
    for k, (source, target) in enumerate(arrays):
        all_ = lead(source)
        for r in range(FOLD + REACH):
            for half, row in ((0, r), (1, ROWS - 1 - r)):
                pltpu.make_async_copy(
                    source.at[all_ + (row // 8, slice(None), row % 8)],
                    target.at[all_ + (REACH + r, pl.ds(4 * half, 4))],
                    local.at[k],
                ).start()

    pl.semaphore_wait(barrier, 2)

    for k, (source, target) in enumerate(arrays):
        all_ = lead(source)
        for r in range(REACH):
            for half, row, to in ((0, ROWS - 1 - r, down), (1, r, up)):
                pltpu.make_async_remote_copy(
                    source.at[all_ + (row // 8, slice(None), row % 8)],
                    target.at[all_ + (REACH - 1 - r, pl.ds(4 * half, 4))],
                    send.at[k, half],
                    recv.at[k, half],
                    device_id={"space": to},
                    device_id_type=MESH,
                ).start()

    for k, (source, target) in enumerate(arrays):
        own = target.at[lead(source) + (pl.ds(REACH, FOLD + REACH),)]
        pltpu.make_async_copy(own, own, local.at[k]).wait()

    def phasors(first, last):
        def one(d, carry):
            for p in range(first, last):
                real, imag = phasor(A[d, p], B[d, p])
                zr[d, p] = real
                zi[d, p] = imag
            return carry

        lax.fori_loop(0, DATES, one, 0)

    phasors(REACH, EXT)
    for p in range(REACH, EXT):
        wt[p] = jnp.where(V[p] == 1, 1.0, MASKED).astype(F32)

    for k, (source, target) in enumerate(arrays):
        for half in range(2):
            edge = target.at[lead(source) + (pl.ds(0, REACH), pl.ds(4 * half, 4))]
            pltpu.make_async_copy(edge, edge, send.at[k, half]).wait()
            pltpu.make_async_copy(edge, edge, recv.at[k, half]).wait()

    phasors(0, REACH)
    above = jnp.where(me > 0, 1.0, 0.0).astype(F32)
    below = jnp.where(me < count - 1, 1.0, 0.0).astype(F32)
    inside = jnp.where(sublanes() < 4, above, below)
    for p in range(REACH):
        wt[p] = jnp.where(V[p] == 1, 1.0, MASKED).astype(F32) * inside


def main_kernel(
    iterations, chosen, zr, zi, wt, linked_r, linked_i, datum, turned_datum,
    wr, wi, inv, R, I, S, QR, QI, QS, QD, vec, band, spill,
    cut, weight, far_weight, strips, links, parts, whole, send, recv, own, back_send, back_recv,
):
    stacks, spaces = lax.axis_size("tm"), lax.axis_size("space")
    m, s = lax.axis_index("tm"), lax.axis_index("space")
    partner = lax.rem(s + spaces // 2, spaces)
    up, down = lax.rem(partner + spaces - 1, spaces), lax.rem(partner + 1, spaces)
    barrier = pltpu.get_barrier_semaphore()

    def greet(k, carry):
        for space in (up, partner, down):
            pl.semaphore_signal(barrier, inc=1, device_id={"tm": k, "space": space}, device_id_type=MESH)
        return carry

    lax.fori_loop(0, stacks, greet, 0)

    band[...] = band_matrix()
    columns = column_sums(band, spill)

    def own_power(k, carry):
        for t in range(2):
            d = 2 * k + t
            values = [wt[p] * (zr[d, p] * zr[d, p] + zi[d, p] * zi[d, p]) for p in range(EXT)]
            for r, total in enumerate(columns(row_sums(values), t)):
                inv[d, r] = 0.5 * lax.rsqrt(total)
        return carry

    lax.fori_loop(0, DATES // 2, own_power, 0)

    def weighted(d, carry):
        for p in range(EXT):
            wr[d, p] = wt[p] * zr[d, p]
            wi[d, p] = wt[p] * zi[d, p]
        return carry

    lax.fori_loop(0, DATES, weighted, 0)

    def matching(turn, carry):
        for t in range(DATES // 2):
            first = lax.rem(turn + t, DATES - 1)
            second = lax.rem(turn + (DATES - 1 - t), DATES - 1) if t else DATES - 1
            i, j = jnp.minimum(first, second), jnp.maximum(first, second)
            real, imag = [], []
            for p in range(EXT):
                a, b, c, d = wr[i, p], wi[i, p], zr[j, p], zi[j, p]
                real.append(a * c + b * d)
                imag.append(b * c - a * d)
            sums = columns(row_sums(real) + row_sums(imag), t)
            for r in range(FOLD):
                scale = inv[i, r] * inv[j, r]
                x = sums[r] * scale
                y = sums[FOLD + r] * scale
                R[r, i * DATES + j] = x
                I[r, i * DATES + j] = y
                S[r, i * DATES + j] = x + y
                S[r, j * DATES + i] = x - y
        return carry

    lax.fori_loop(0, DATES - 1, matching, 0)

    windows = column_windows()
    for p in range(REACH + FOLD):
        for q, window in enumerate(windows(wt[p], wt[p])):
            weight[p, 4 * q : 4 * q + 4] = window[:4]
            weight[ROWS + 2 * REACH - 1 - p, 4 * q : 4 * q + 4] = window[4:]

    pl.semaphore_wait(barrier, 3 * stacks)
    weights = pltpu.make_async_remote_copy(
        weight.at[:, m], far_weight, *own, device_id={"space": partner}, device_id_type=MESH
    )
    weights.start()

    n = iterations[0]
    odd = (n & 1) == 1
    turns = (n - 1) >> 1
    ref = chosen[0]

    def flat(i, j):
        return i * DATES + j

    def upper(i, j):
        return flat(min(i, j), max(i, j))

    def row_total(real, imag, diagonal):
        out_r, out_i = [], []
        for i in range(DATES):
            tr, ti = diagonal(i), None
            for j in range(DATES):
                if j == i:
                    continue
                tr = tr + real(upper(i, j))
                value = imag(upper(i, j))
                if ti is None:
                    ti = value if i < j else -value
                else:
                    ti = ti + value if i < j else ti - value
            out_r.append(tr)
            out_i.append(ti)
        return out_r, out_i

    def position(r, carry):
        squares = [jnp.full((8, 128), 0.25, F32) for _ in range(DATES)]
        for i in range(DATES):
            for j in range(i + 1, DATES):
                k = flat(i, j)
                x, y = R[r, k], I[r, k]
                size = x * x + y * y
                squares[i] = squares[i] + size
                squares[j] = squares[j] + size
        for i in range(DATES):
            QD[i] = squares[i]
        for i in range(DATES):
            for j in range(i + 1, DATES):
                rr, ii, mixed = None, None, None
                for k in range(DATES):
                    if k == i or k == j:
                        continue
                    a = R[r, upper(i, k)] * R[r, upper(j, k)]
                    b = I[r, upper(i, k)] * I[r, upper(j, k)]
                    c = S[r, flat(i, k)] * S[r, flat(k, j)]
                    same = (i < k) == (j < k)
                    rr = a if rr is None else rr + a
                    if ii is None:
                        ii = b if same else -b
                    else:
                        ii = ii + b if same else ii - b
                    mixed = c if mixed is None else mixed + c
                k = flat(i, j)
                x = R[r, k] + (rr + ii)
                y = I[r, k] + (mixed - (rr - ii))
                QR[k] = x
                QI[k] = y
                QS[k] = x + y
                QS[flat(j, i)] = x - y

        one_r, one_i = row_total(lambda k: R[r, k], lambda k: I[r, k], lambda i: jnp.full((8, 128), 0.5, F32))
        two_r, two_i = row_total(lambda k: QR[k], lambda k: QI[k], lambda i: QD[i])
        start = [jnp.where(odd, a, b) for a, b in zip(one_r + one_i, two_r + two_i)]

        def turn(count, v):
            vr, vi = v[:DATES], v[DATES:]
            both = [a + b for a, b in zip(vr, vi)]
            out_r, out_i = [], []
            for i in range(DATES):
                d = QD[i]
                rr, ii, mixed = None, None, None
                for j in range(DATES):
                    if j == i:
                        continue
                    a = QR[upper(i, j)] * vr[j]
                    b = QI[upper(i, j)] * vi[j]
                    c = QS[flat(i, j)] * both[j]
                    rr = a if rr is None else rr + a
                    if ii is None:
                        ii = b if i < j else -b
                    else:
                        ii = ii + b if i < j else ii - b
                    mixed = c if mixed is None else mixed + c
                out_r.append(d * vr[i] + (rr - ii))
                out_i.append(d * vi[i] + (mixed - (rr + ii)))
            return out_r + out_i

        def maybe(count, v):
            return [jnp.where(count < turns, a, b) for a, b in zip(turn(count, v), v)]

        v = lax.fori_loop(0, LEAST_TURNS, turn, start)
        v = lax.fori_loop(LEAST_TURNS, MOST_TURNS, maybe, v)
        total = None
        for x in v:
            total = x * x if total is None else total + x * x
        scale = lax.rsqrt(total)
        v = [x * scale for x in v]
        vr, vi = v[:DATES], v[DATES:]
        for t in range(2 * DATES):
            vec[t] = v[t]
        cr, ci = None, None
        for t in range(DATES):
            a, b = zr[t, r + REACH], zi[t, r + REACH]
            x = vr[t] * a + vi[t] * b
            y = vr[t] * b - vi[t] * a
            cr = x if cr is None else cr + x
            ci = y if ci is None else ci + y
        for q, window in enumerate(windows(cr, ci)):
            cut[r, 4 * q : 4 * q + 4] = window[:4]
            cut[ROWS - 1 - r, 4 * q : 4 * q + 4] = window[4:]
        ref_r, ref_i = DATES * vec[ref], DATES * vec[DATES + ref]
        for t in range(DATES):
            x = vr[t] * ref_r + vi[t] * ref_i
            y = vi[t] * ref_r - vr[t] * ref_i
            for target, value in ((linked_r, x), (linked_i, y)):
                for half, row in ((0, r), (1, ROWS - 1 - r)):
                    first = (row >> 3) * 32 + (row & 7)
                    target[t, pl.ds(first, 4, stride=8), :] = value[4 * half : 4 * half + 4]
        for last, pieces in STAGES:

            @pl.when(r == last)
            def _():
                lax.fori_loop(0, stacks, lambda k, c: share(lax.rem(m + k, stacks), c, pieces), 0)

        return carry

    def share(k, carry, pieces):
        def start(first, size, to, space):
            pltpu.make_async_remote_copy(
                cut.at[pl.ds(first, size), k],
                strips.at[pl.ds(to, size), m],
                send,
                recv,
                device_id={"tm": k, "space": space},
                device_id_type=MESH,
            ).start()

        for first, size in pieces:

            start(first, size, REACH + first, partner)
        if not pieces:
            start(0, REACH, REACH + ROWS, up)
            start(ROWS - REACH, REACH, 0, down)
        return carry

    lax.fori_loop(0, FOLD, position, 0)

    weights.wait()
    pltpu.make_async_copy(strips, strips, recv).wait()
    lane, sub = lanes(), sublanes()
    halves = (pl.ds(0, 8), pl.ds(8, 8))

    def next_stack(pair):
        second = pltpu.roll(pair[1], 7, 0)
        return jnp.where(sub < 7, pltpu.roll(pair[0], 7, 0), second), second

    low, middle, left = lane < THIRD, lane < 2 * THIRD, lane < 64
    fields = ([], [])
    for p in range(ROWS + 2 * REACH):
        w = jnp.broadcast_to(far_weight[pl.ds(p, 1)], (8, 128))
        pair = [strips[p, half] for half in halves]
        for field, x, y in zip(fields, pair, next_stack(pair)):
            straight = x * y
            crossed = x * pltpu.roll(y, 128 - THIRD, 1)
            power = x * x
            value = jnp.where(
                low,
                straight + pltpu.roll(straight, 128 - THIRD, 1),
                jnp.where(
                    middle, crossed - pltpu.roll(crossed, THIRD, 1), power + pltpu.roll(power, THIRD, 1)
                ),
            )
            field.append(w * value)
    sums = [long_row_sums(field) for field in fields]
    for r in range(ROWS):
        pair = []
        for half in range(2):
            x = sums[half][r]
            for amount in (127, 126, 125, 124):
                x = x + pltpu.roll(sums[half][r], amount, 1)
            pair.append(x)
        for half, x, y in zip(halves, pair, next_stack(pair)):
            scale = lax.rsqrt((x + 1.0) * (y + 1.0))
            x = x * jnp.where(low, pltpu.roll(scale, 128 - 2 * THIRD, 1), pltpu.roll(scale, 128 - THIRD, 1))
            size = x * x
            size = size + jnp.where(low, pltpu.roll(size, 128 - THIRD, 1), pltpu.roll(size, THIRD, 1))
            first = 16 * r + (half.start)
            links[pl.ds(first, 8)] = x * lax.rsqrt(jnp.maximum(size, FLOOR * FLOOR))

    xr = [jnp.ones((8, 128), F32)] * TILES
    xi = [jnp.zeros((8, 128), F32)] * TILES
    for k in range(stacks):
        tiles = [jnp.where(lane < 32, xr[t], pltpu.roll(xi[t], 32, 1)) for t in range(TILES)]
        parts[k, 0:8] = jnp.where(left, tiles[0], pltpu.roll(tiles[1], 64, 1))
        parts[k, 8:16] = jnp.where(left, tiles[2], pltpu.roll(pltpu.roll(tiles[2], 64, 1), 4, 0))
        pltpu.make_async_remote_copy(
            parts.at[k, pl.ds(0, 12)],
            whole.at[m, pl.ds(0, 12)],
            back_send,
            back_recv,
            device_id={"tm": k, "space": partner},
            device_id_type=MESH,
        ).start()
        if k < stacks - 1:
            for t in range(TILES):
                lr = links[pl.ds(128 * t + k, 8, stride=16)]
                li = pltpu.roll(lr, 128 - THIRD, 1)
                xr[t], xi[t] = xr[t] * lr - xi[t] * li, xr[t] * li + xi[t] * lr
    most = whole.at[:, pl.ds(0, 12)]
    pltpu.make_async_copy(most, most, back_recv).wait()

    for b in range(4):
        joined = [None] * 6
        for q in range(4):
            x, y = whole[4 * q + b, 0:8], whole[4 * q + b, 8:16]
            y = jnp.where(sub < 4, y, pltpu.roll(pltpu.roll(y, 64, 1), 4, 0))
            for n in range(6):
                source, quarter = (x, n) if n < 4 else (y, n - 4)
                amount = 32 * (q - quarter) % 128
                turned = pltpu.roll(source, amount, 1) if amount else source
                joined[n] = turned if q == 0 else jnp.where(lane < 32 * q, joined[n], turned)
        for t in range(TILES):
            rows = pl.ds(8 * (4 * t + b), 8)
            datum[0, rows] = joined[2 * t]
            datum[1, rows] = joined[2 * t + 1]
            turned_datum[0, rows] = -joined[2 * t + 1]
            turned_datum[1, rows] = joined[2 * t]
    pltpu.make_async_copy(strips, strips, send).wait()
    pltpu.make_async_copy(most, most, back_send).wait()


def vmem():
    return pl.BlockSpec(memory_space=pltpu.VMEM)


def smem():
    return pl.BlockSpec(memory_space=pltpu.SMEM)


def hbm():
    return pl.BlockSpec(memory_space=pltpu.HBM)


def shape(*dims):
    return jax.ShapeDtypeStruct(dims, F32)


def scratch(*dims):
    return pltpu.VMEM(dims, F32)


def tiled(x):
    lead = x.shape[:-2]
    k = len(lead)
    return x.reshape(lead + (TILES, 8, 4, 128)).transpose(tuple(range(k)) + (k, k + 2, k + 1, k + 3))


def local(amplitude, phase, validity, iterations, reference_date):
    dma = pltpu.SemaphoreType.DMA
    zr, zi, wt = pl.pallas_call(
        halo_kernel,
        out_shape=[shape(DATES, EXT, 8, 128), shape(DATES, EXT, 8, 128), shape(EXT, 8, 128)],
        in_specs=[hbm()] * 3,
        out_specs=[vmem()] * 3,
        scratch_shapes=[
            scratch(DATES, EXT, 8, 128),
            scratch(DATES, EXT, 8, 128),
            pltpu.VMEM((EXT, 8, 128), jnp.int32),
            dma((3,)),
            dma((3, 2)),
            dma((3, 2)),
        ],
        compiler_params=pltpu.CompilerParams(
            collective_id=0, has_side_effects=True, vmem_limit_bytes=16 << 20
        ),
        name="halo",
    )(*[pltpu.with_memory_space_constraint(tiled(x), pltpu.HBM) for x in (amplitude, phase, validity)])
    linked_r, linked_i, datum, turned = pl.pallas_call(
        main_kernel,
        out_shape=[shape(DATES, 4 * ROWS, 128)] * 2 + [shape(2, 4 * ROWS, 128)] * 2,
        in_specs=[smem(), smem(), vmem(), vmem(), vmem()],
        out_specs=[vmem()] * 4,
        scratch_shapes=[
            scratch(DATES, EXT, 8, 128),
            scratch(DATES, EXT, 8, 128),
            scratch(DATES, FOLD, 8, 128),
            scratch(FOLD, DATES * DATES, 8, 128),
            scratch(FOLD, DATES * DATES, 8, 128),
            scratch(FOLD, DATES * DATES, 8, 128),
            scratch(DATES * DATES, 8, 128),
            scratch(DATES * DATES, 8, 128),
            scratch(DATES * DATES, 8, 128),
            scratch(DATES, 8, 128),
            scratch(2 * DATES, 8, 128),
            pltpu.VMEM((256, 256), jnp.bfloat16),
            scratch(DATES // 2, 16 * FOLD + 16, 128),
            scratch(ROWS, 16, 128),
            scratch(ROWS + 2 * REACH, 16, 128),
            scratch(ROWS + 2 * REACH, 128),
            scratch(ROWS + 2 * REACH, 16, 128),
            scratch(16 * ROWS, 128),
            scratch(16, 16, 128),
            scratch(16, 16, 128),
            dma(()),
            dma(()),
            [dma(()), dma(())],
            dma(()),
            dma(()),
        ],
        compiler_params=pltpu.CompilerParams(
            collective_id=1, has_side_effects=True, vmem_limit_bytes=40 << 20
        ),
        name="power",
    )(iterations, reference_date, zr, zi, wt)
    out = linked_r * datum[:, None] + linked_i * turned[:, None]
    out = out.reshape(2, DATES, TILES, 4, 8, 128).transpose(0, 1, 2, 4, 3, 5)
    return out.reshape(2, DATES, ROWS, 512)


def solution(mesh):
    return jax.shard_map(
        local,
        mesh=mesh,
        in_specs=(P("tm", "space", None), P("tm", "space", None), P("space", None), P("tm"), P("tm")),
        out_specs=P(None, "tm", "space", None),
        check_vma=False,
    )
```
